128 devices in a mesh: blk: 32 (over z, y, core), col: 4 (over x).
Axes of the slice: x: 4, y: 4, z: 4, core: 2. Of those that a mesh axis runs over, the one named last changes fastest.
Arguments:
- rank_in: float32 [4096, 512], P(('blk', 'col')), may hold values from 0.5 to 1.5
- delta_in: float32 [4096, 512], P(('blk', 'col'))
- out_degree: int32 [4096, 512], P(('blk', 'col')), may hold values from 98 to 194
- tile_weight: bfloat16 [4096, 512, 512], P(('blk', 'col'))
- tile_source: int32 [4096], P(('blk', 'col')), may hold values from 0 to 1023, as said below
- tile_row: int32 [4096], P(('blk', 'col')), may hold values from 0 to 127
- tile_valid: int32 [4096], P(('blk', 'col')), may hold values 0 or 1
Outputs:
- rank_out: float32 [4096, 512], P(('blk', 'col'))
- delta_out: float32 [4096, 512], P(('blk', 'col'))
- masses: float32 [6], replicated
The draws below stay inside these ranges and needn't reach their ends.
Inputs may be any that keep to these rules, and one draw needn't show every extreme that they name: `tile_source`: slot j of the 32 slots of each device (tiles i with i % 32 = j) names a source block from 32 * j to 32 * j + 31.
All inputs are finite; a program needn't handle non-finite values. No bound on the sum of `tile_valid` on one device may be relied on, other than what follows from the above.
Results may differ from the reference program's by a relative error of at most 0.00039.
Values may be sent and summed in bfloat16 or wider, within the bound.
No kernel may reach another device: no remote copies, remote signals or barrier semaphores. Data moves between devices by JAX's collectives and lax.ppermute only.
A program may use at most 64 MiB of HBM per device.

```python
import jax
import jax.numpy as jnp
from jax import lax

BLOCK = 512
VB = 32
ITERS = 6
NB = 4096
TILES = 4096
N_BLK = 32
N_COL = 4


def draw_delta_in(key, part):
    first, second = jax.random.split(jax.random.fold_in(key, 11))
    place = jnp.arange(NB, dtype=jnp.float32) / NB
    rise = 1.0 + 2.0 * place
    rough = jax.random.uniform(second, (NB, 1), jnp.float32, 0.5, 1.5)
    base = jax.random.normal(first, (NB, BLOCK), jnp.float32) + 0.5
    return base * rise[:, None] * rough


def draw_tile_weight(key, part):
    first, second = jax.random.split(jax.random.fold_in(key, 23))
    links = jax.random.bernoulli(first, 0.5, (TILES, BLOCK, BLOCK)).astype(jnp.float32)
    values = jax.random.uniform(second, (TILES, BLOCK, BLOCK), jnp.float32, 0.2, 1.0)
    return (links * values).astype(jnp.bfloat16)


def draw_tile_source(key, part):
    slots = jnp.arange(TILES, dtype=jnp.int32) % N_BLK
    offset = jax.random.randint(jax.random.fold_in(key, 37), (TILES,), 0, VB).astype(jnp.int32)
    return slots * VB + offset


def touch_ends(values, rng, least, high):
    longest = values.shape.index(max(values.shape))
    spots = []
    for shift in (0, 1):
        where = [jax.random.randint(jax.random.fold_in(rng, axis), (), 0, length) for axis, length in enumerate(values.shape)]
        where[longest] = (where[longest] + shift) % values.shape[longest]
        spots.append(tuple(where))
    return values.at[spots[0]].set(least).at[spots[1]].set(high)


def steps_of(rng, shape, cuts, smallest, high):
    gain, own = 1.0, jax.random.fold_in(rng, 6)
    for position, shards_of in cuts:
        heights = jnp.exp(jax.random.uniform(jax.random.fold_in(own, position), (shards_of,), jnp.float32, smallest / len(cuts), high / len(cuts)))
        gain = gain * jnp.repeat(heights, shape[position] // shards_of).reshape([-1 if axis == position else 1 for axis in range(len(shape))])
    return gain


def setup_inputs(seed: int = 0) -> dict:
    seeds = jax.random.split(jax.random.key(seed), 8)
    return {
        "rank_in": jnp.clip(0.5 + 1.0 * jax.random.uniform(seeds[0], (NB, BLOCK), jnp.float32) ** steps_of(seeds[0], (NB, BLOCK), ((0, 128),), -0.2, 0.2), 0.5, 1.5),
        "delta_in": draw_delta_in(jax.random.fold_in(seeds[7], 71), 0),
        "out_degree": touch_ends(jax.random.randint(seeds[2], (NB, BLOCK), 3 * BLOCK * N_BLK // (16 * VB) + 2, 3 * BLOCK * N_BLK // (8 * VB) + 3), jax.random.fold_in(seeds[2], 1), 3 * BLOCK * N_BLK // (16 * VB) + 2, (3 * BLOCK * N_BLK // (8 * VB) + 3) - 1).astype(jnp.int32),
        "tile_weight": draw_tile_weight(jax.random.fold_in(seeds[7], 71), 0),
        "tile_source": draw_tile_source(jax.random.fold_in(seeds[7], 71), 0),
        "tile_row": touch_ends(jax.random.randint(seeds[5], (TILES,), 0, N_COL * VB), jax.random.fold_in(seeds[5], 1), 0, (N_COL * VB) - 1).astype(jnp.int32),
        "tile_valid": touch_ends((jax.random.randint(seeds[6], (TILES,), 0, 4) < 3).astype(jnp.int32), jax.random.fold_in(seeds[6], 1), 0, 1),
    }


damping = 0.85


def reference(rank_in, delta_in, out_degree, tile_weight, tile_source, tile_row, tile_valid):
    slots = jnp.arange(TILES, dtype=jnp.int32)
    device = slots // N_BLK
    group = device // N_COL
    column = device % N_COL
    dest = (group * (N_COL * VB) + tile_row).astype(jnp.int32)
    src = ((tile_source // VB) * (N_COL * VB) + column * VB + tile_source % VB).astype(jnp.int32)
    scale = damping / out_degree.astype(jnp.float32)
    valid = tile_valid.astype(jnp.float32)
    delta = delta_in
    total = rank_in
    masses = []
    for step in range(ITERS):
        masses.append(jnp.sum(jnp.abs(delta)) / (NB * BLOCK))
        total = total + delta
        contrib = (delta * scale).astype(jnp.bfloat16)

        def one_tile(items):
            tile, source = items
            vector = contrib[source].astype(jnp.float32)
            return jnp.dot(tile.astype(jnp.float32), vector, precision=lax.Precision.HIGHEST)

        products = lax.map(one_tile, (tile_weight, src))
        products = products * valid[:, None]
        delta = jnp.zeros((NB, BLOCK), jnp.float32).at[dest].add(products)
    return total, delta, jnp.stack(masses)
```

```python
import functools

import jax
import jax.numpy as jnp
from jax import lax
from jax.experimental import pallas as pl
from jax.experimental.pallas import tpu as pltpu
from jax.sharding import Mesh
from jax.sharding import PartitionSpec as P

ITERS = 6
BLK = ("blk_0", "blk_1", "blk_2")
BLK_COL = ("blk_0", "blk_1", "blk_2", "col")
LANES = 128
GROUP = 8

damping = 0.85

VMEM = pl.BlockSpec(memory_space=pltpu.VMEM)
SMEM = pl.BlockSpec(memory_space=pltpu.SMEM)


def lane_row(column):
    rows = lax.broadcasted_iota(jnp.int32, column.shape, 0)
    lanes = lax.broadcasted_iota(jnp.int32, column.shape, 1)
    return jnp.sum(jnp.where(rows == lanes, column, 0.0), axis=0, keepdims=True)


def pieces(value):
    high = value.astype(jnp.bfloat16).astype(jnp.float32)
    rest = value - high
    middle = rest.astype(jnp.bfloat16).astype(jnp.float32)
    low = (rest - middle).astype(jnp.bfloat16).astype(jnp.float32)
    return high, middle, low


def plan_kernel(cols, me, row, valid, order, place, count):
    tiles = row.shape[0]
    owned = tiles
    c = me[0]

    def live(i, n):
        target = lax.rem(row[i] // owned + cols - c, cols) * owned + lax.rem(row[i], owned)
        place[i] = target

        @pl.when(valid[i] != 0)
        def _():
            order[n] = i

        return n + (valid[i] != 0).astype(jnp.int32)

    n = lax.fori_loop(0, tiles, live, jnp.int32(0))
    count[0] = n

    def rest(i, m):
        @pl.when(valid[i] == 0)
        def _():
            order[m] = i

        return m + (valid[i] == 0).astype(jnp.int32)

    lax.fori_loop(0, tiles, rest, n)


def send(asked, owned, contrib, message, extra):
    for b in range(asked.shape[0]):
        block = contrib[lax.rem(asked[b], owned)]
        if extra is None:
            message[b, 0:4, :] = block.astype(jnp.bfloat16)
        else:
            message[b] = jnp.concatenate([block, extra], axis=0).astype(jnp.bfloat16)


def first_kernel(asked, delta_in, rank_in, degree, message, scale, total, masses, contrib):
    owned = delta_in.shape[0]
    mass = jnp.zeros((1, LANES), jnp.float32)
    for r in range(4):
        part = slice(LANES * r, LANES * (r + 1))
        delta = delta_in[:, part]
        factor = damping / degree[:, part].astype(jnp.float32)
        scale[:, r, :] = factor
        total[:, r, :] = rank_in[:, part] + delta
        contrib[:, r, :] = (delta * factor)
        mass = mass + jnp.sum(jnp.abs(delta), axis=0, keepdims=True)
    masses[...] = jnp.concatenate([mass, jnp.zeros((7, LANES), jnp.float32)], axis=0)
    send(asked, owned, contrib, message, None)


def join_kernel(step, cells, asked, own, one, two, three, scale, total, masses, *rest):
    message, total_out, masses_out, contrib = rest
    owned = own.shape[0]
    delta = own[...] + one[...] + two[...] + three[...]
    total_out[...] = total[...] + delta
    contrib[...] = delta * scale[...]
    mass = jnp.sum(jnp.sum(jnp.abs(delta), axis=0), axis=0, keepdims=True)
    rows = lax.broadcasted_iota(jnp.int32, (8, LANES), 0)
    merged = jnp.where(rows == step, mass, masses[...])
    masses_out[...] = merged
    extra = None
    if step == ITERS - 1:
        sums = jnp.broadcast_to(jnp.sum(merged, axis=1, keepdims=True) / cells, (8, LANES))
        extra = jnp.concatenate([*pieces(lane_row(sums)), jnp.zeros((1, LANES), jnp.float32)], axis=0)
    send(asked, owned, contrib, message, extra)


def tile_kernel(last, order, place, count, picked, weight, own, one, two, three, vectors, sums):
    owned = weight.shape[0]
    sums[...] = jnp.zeros_like(sums)
    vectors[...] = picked[...].astype(jnp.float32)
    rows = lax.broadcasted_iota(jnp.int32, (8, LANES), 0)

    def group(g, carry):
        products = []
        for u in range(GROUP):
            i = g * GROUP + u
            j = order[i]
            live = jnp.where(i < count[0], 1.0, 0.0)
            wide = jnp.concatenate(
                [jnp.broadcast_to(vectors[j, r : r + 1, :], (8, LANES)) for r in range(4)], axis=1
            )
            product = lax.dot_general(
                (wide * live).astype(jnp.bfloat16),
                weight[j],
                (((1,), (1,)), ((), ())),
                preferred_element_type=jnp.float32,
            )
            block = product[:, 3 * LANES :]
            for r in (2, 1, 0):
                block = jnp.where(rows == r, product[:, LANES * r : LANES * (r + 1)], block)
            products.append((j, block))
        for j, block in products:
            q = place[j]
            sums[q] = sums[q] + block[:4]
        return carry

    lax.fori_loop(0, (count[0] + GROUP - 1) // GROUP, group, 0)
    for s, out in enumerate((own, one, two, three)):
        out[0:owned] = sums[s * owned : (s + 1) * owned]
    if last:
        mass = jnp.zeros((1, LANES), jnp.float32)
        for r in (4, 5, 6):
            mass = mass + jnp.sum(vectors[:, r, :], axis=0, keepdims=True)
        for out in (own, one, two, three):
            out[owned] = jnp.broadcast_to(mass, (4, LANES))


def last_kernel(me, own, one, two, three, total, rank_out, delta_out, masses, ordered):
    owned = total.shape[0]
    for r in range(4):
        part = slice(LANES * r, LANES * (r + 1))
        rank_out[:, part] = total[:, r, :]
        delta_out[:, part] = (
            own[0:owned, r, :] + one[0:owned, r, :] + two[0:owned, r, :] + three[0:owned, r, :]
        )
    for s, part in enumerate((own, one, two, three)):
        ordered[lax.rem(me[0] + 4 - s, 4)] = part[owned]
    masses[...] = (ordered[0] + ordered[1] + ordered[2] + ordered[3])[0:1]


def f32(*shape):
    return jax.ShapeDtypeStruct(shape, jnp.float32)


def s32(*shape):
    return jax.ShapeDtypeStruct(shape, jnp.int32)


def call(kernel, outs, specs_in, specs_out, scratch, vmem=8):
    return pl.pallas_call(
        kernel,
        out_shape=outs,
        in_specs=specs_in,
        out_specs=specs_out,
        scratch_shapes=scratch,
        compiler_params=pltpu.CompilerParams(vmem_limit_bytes=vmem << 20),
    )


def on_device(rank_in, delta_in, out_degree, tile_weight, tile_source, tile_row, tile_valid):
    owned, width = delta_in.shape
    tiles = tile_row.shape[0]
    n_group = lax.axis_size(BLK)
    n_column = lax.axis_size("col")
    cells = owned * n_group * n_column * width
    me = lax.axis_index("col").astype(jnp.int32).reshape(1)
    asked = lax.all_to_all(
        tile_source.reshape(n_group, 1), BLK, split_axis=0, concat_axis=0, tiled=True
    ).reshape(n_group)
    order, place, count = call(
        functools.partial(plan_kernel, n_column),
        (s32(tiles), s32(tiles), s32(1)),
        [SMEM] * 3,
        (SMEM,) * 3,
        [],
    )(me, tile_row, tile_valid)
    held = f32(owned, 4, LANES)
    message = jax.ShapeDtypeStruct((n_group, 8, LANES), jnp.bfloat16)
    block_scratch = pltpu.VMEM((owned, 4, LANES), jnp.float32)
    out, scale, total, masses = call(
        first_kernel,
        (message, held, held, f32(8, LANES)),
        [SMEM] + [VMEM] * 3,
        (VMEM,) * 4,
        [block_scratch],
    )(asked, delta_in, rank_in, out_degree)
    for step in range(ITERS):
        picked = lax.all_to_all(out, BLK, split_axis=0, concat_axis=0, tiled=True)
        last = step == ITERS - 1
        sent = f32(owned + last, 4, LANES)
        parts = call(
            functools.partial(tile_kernel, last),
            (sent,) * 4,
            [SMEM] * 3 + [VMEM] * 2,
            (VMEM,) * 4,
            [
                pltpu.VMEM((tiles, 8, LANES), jnp.float32),
                pltpu.VMEM((n_column * owned, 4, LANES), jnp.float32),
            ],
            vmem=24,
        )(order, place, count, picked, tile_weight)
        own, others = parts[0], parts[1:]
        others = [
            lax.ppermute(part, "col", [(i, (i + s + 1) % n_column) for i in range(n_column)])
            for s, part in enumerate(others)
        ]
        if not last:
            out, total, masses = call(
                functools.partial(join_kernel, step + 1, cells),
                (message, held, f32(8, LANES)),
                [SMEM] + [VMEM] * 7,
                (VMEM,) * 3,
                [block_scratch],
            )(asked, own, *others, scale, total, masses)
    rank_out, delta_out, stacked = call(
        last_kernel,
        (f32(owned, width), f32(owned, width), f32(1, LANES)),
        [SMEM] + [VMEM] * 5,
        (VMEM,) * 3,
        [pltpu.VMEM((4, 4, LANES), jnp.float32)],
    )(me, own, *others, total)
    return rank_out, delta_out, stacked[0, :ITERS]


def solution(mesh):
    finer = Mesh(
        mesh.devices.reshape(4, 4, 2, mesh.shape["col"]), ("blk_0", "blk_1", "blk_2", "col")
    )
    placed = (
        P(BLK_COL, None),
        P(BLK_COL, None),
        P(BLK_COL, None),
        P(BLK_COL, None, None),
        P(BLK_COL),
        P(BLK_COL),
        P(BLK_COL),
    )
    return jax.shard_map(
        on_device,
        mesh=finer,
        in_specs=placed,
        out_specs=(P(BLK_COL, None), P(BLK_COL, None), P()),
        check_vma=False,
    )
```

```python
import functools

import jax
import jax.numpy as jnp
from jax import lax
from jax.experimental import pallas as pl
from jax.experimental.pallas import tpu as pltpu
from jax.sharding import Mesh
from jax.sharding import PartitionSpec as P

ITERS = 6
BLK = ("blk_0", "blk_1", "blk_2")
BLK_COL = ("blk_0", "blk_1", "blk_2", "col")
LANES = 128
GROUP = 16
FIRST_GROUP = 4
EARLY = 20

damping = 0.85

VMEM = pl.BlockSpec(memory_space=pltpu.VMEM)
SMEM = pl.BlockSpec(memory_space=pltpu.SMEM)
HBM = pl.BlockSpec(memory_space=pltpu.HBM)


def lane_row(column):
    rows = lax.broadcasted_iota(jnp.int32, column.shape, 0)
    lanes = lax.broadcasted_iota(jnp.int32, column.shape, 1)
    return jnp.sum(jnp.where(rows == lanes, column, 0.0), axis=0, keepdims=True)


def pieces(value):
    high = value.astype(jnp.bfloat16).astype(jnp.float32)
    rest = value - high
    middle = rest.astype(jnp.bfloat16).astype(jnp.float32)
    low = (rest - middle).astype(jnp.bfloat16).astype(jnp.float32)
    return high, middle, low


def plan(cols, c, row, valid, table):
    tiles = row.shape[0]
    owned = tiles

    def live(i, n):
        table[tiles + i] = lax.rem(row[i] // owned + cols - c, cols) * owned + lax.rem(row[i], owned)
        table[3 * tiles + i] = valid[i]

        @pl.when(valid[i] != 0)
        def _():
            table[n] = i

        return n + (valid[i] != 0).astype(jnp.int32)

    n = lax.fori_loop(0, tiles, live, jnp.int32(0))
    table[2 * tiles] = n

    def rest(i, m):
        @pl.when(valid[i] == 0)
        def _():
            table[m] = i

        return m + (valid[i] == 0).astype(jnp.int32)

    lax.fori_loop(0, tiles, rest, n)


def send(asked, owned, contrib, message, extra):
    for b in range(asked.shape[0]):
        block = contrib[lax.rem(asked[b, 0, 0], owned)]
        if extra is None:
            message[b, 0:4, :] = block.astype(jnp.bfloat16)
        else:
            message[b] = jnp.concatenate([block, extra], axis=0).astype(jnp.bfloat16)


def stage_kernel(cols, *refs):
    me, delta_hbm, rank_hbm, degree_hbm, row_hbm, valid_hbm = refs[:6]
    table, scale, total, masses, contrib = refs[6:11]
    delta_in, rank_in, degree, row, valid, sems = refs[11:]
    copies = [
        pltpu.make_async_copy(source, target, sems.at[i])
        for i, (source, target) in enumerate(
            (
                (row_hbm, row),
                (valid_hbm, valid),
                (delta_hbm, delta_in),
                (rank_hbm, rank_in),
                (degree_hbm, degree),
            )
        )
    ]
    for copy in copies:
        copy.start()
    for copy in copies:
        copy.wait()
    plan(cols, me[0], row, valid, table)
    mass = jnp.zeros((1, LANES), jnp.float32)
    for r in range(4):
        part = slice(LANES * r, LANES * (r + 1))
        delta = delta_in[:, part]
        factor = damping / degree[:, part].astype(jnp.float32)
        scale[:, r, :] = factor
        total[:, r, :] = rank_in[:, part] + delta
        contrib[:, r, :] = delta * factor
        mass = mass + jnp.sum(jnp.abs(delta), axis=0, keepdims=True)
    masses[...] = jnp.concatenate([mass, jnp.zeros((7, LANES), jnp.float32)], axis=0)


def turn_kernel(low, high, *refs):
    weight, turned, mark = refs[0], refs[-2], refs[-1]
    mark[...] = jnp.zeros_like(mark)

    def turn(i, carry):
        turned[low + 2 * i] = weight[low + 2 * i].T
        turned[low + 2 * i + 1] = weight[low + 2 * i + 1].T
        return carry

    lax.fori_loop(0, (high - low) // 2, turn, 0)


def first_kernel(asked, contrib, message):
    send(asked, contrib.shape[0], contrib, message, None)


def join_kernel(step, cells, asked, own, one, two, three, scale, total, masses, *rest):
    message, total_out, masses_out, contrib = rest[-4:]
    owned = own.shape[0]
    delta = own[...] + one[...] + two[...] + three[...]
    total_out[...] = total[...] + delta
    contrib[...] = delta * scale[...]
    mass = jnp.sum(jnp.sum(jnp.abs(delta), axis=0), axis=0, keepdims=True)
    rows = lax.broadcasted_iota(jnp.int32, (8, LANES), 0)
    merged = jnp.where(rows == step, mass, masses[...])
    masses_out[...] = merged
    extra = None
    if step == ITERS - 1:
        sums = jnp.broadcast_to(jnp.sum(merged, axis=1, keepdims=True) / cells, (8, LANES))
        extra = jnp.concatenate([*pieces(lane_row(sums)), jnp.zeros((1, LANES), jnp.float32)], axis=0)
    send(asked, owned, contrib, message, extra)


def product(vectors, rows, j, live, weight, contracted):
    wide = jnp.concatenate(
        [jnp.broadcast_to(vectors[j, r : r + 1, :], (8, LANES)) for r in range(4)], axis=1
    )
    found = lax.dot_general(
        (wide * live).astype(jnp.bfloat16),
        weight,
        (((1,), (contracted,)), ((), ())),
        preferred_element_type=jnp.float32,
    )
    block = found[:, 3 * LANES :]
    for r in (2, 1, 0):
        block = jnp.where(rows == r, found[:, LANES * r : LANES * (r + 1)], block)
    return block[:4]


def start_tile_kernel(turn, table, picked, weight_hbm, own, one, two, three, weight, turned, vectors, sums, sems):
    owned = tiles = picked.shape[0]

    def fetch(j):
        return pltpu.make_async_copy(weight_hbm.at[j], weight.at[j], sems.at[j])

    for j in range(tiles):
        fetch(j).start()
    sums[...] = jnp.zeros_like(sums)
    vectors[...] = picked[...].astype(jnp.float32)
    rows = lax.broadcasted_iota(jnp.int32, (8, LANES), 0)

    def group(turning, g, carry):
        found = []
        for u in range(FIRST_GROUP):
            j = g * FIRST_GROUP + u
            fetch(j).wait()
            tile = weight[j]
            if turning:
                turned[j] = tile.T
            live = table[3 * tiles + j].astype(jnp.float32)
            found.append((j, product(vectors, rows, j, live, tile, 1)))
        for j, block in found:
            q = table[tiles + j]
            sums[q] = sums[q] + block
        return carry

    lax.fori_loop(0, turn // FIRST_GROUP, functools.partial(group, True), 0)
    lax.fori_loop(turn // FIRST_GROUP, tiles // FIRST_GROUP, functools.partial(group, False), 0)
    for s, out in enumerate((own, one, two, three)):
        out[...] = sums[s * owned : (s + 1) * owned]


def tile_kernel(last, table, picked, turned, own, one, two, three, vectors, sums):
    owned = tiles = picked.shape[0]
    count = table[2 * tiles]
    sums[...] = jnp.zeros_like(sums)
    vectors[...] = picked[...].astype(jnp.float32)
    rows = lax.broadcasted_iota(jnp.int32, (8, LANES), 0)

    def group(g, carry):
        found = []
        for u in range(GROUP):
            i = g * GROUP + u
            j = table[i]
            live = jnp.where(i < count, 1.0, 0.0)
            found.append((j, product(vectors, rows, j, live, turned[j], 0)))
        for j, block in found:
            q = table[tiles + j]
            sums[q] = sums[q] + block
        return carry

    lax.fori_loop(0, (count + GROUP - 1) // GROUP, group, 0)
    for s, out in enumerate((own, one, two, three)):
        out[0:owned] = sums[s * owned : (s + 1) * owned]
    if last:
        mass = jnp.zeros((1, LANES), jnp.float32)
        for r in (4, 5, 6):
            mass = mass + jnp.sum(vectors[:, r, :], axis=0, keepdims=True)
        for out in (own, one, two, three):
            out[owned] = jnp.broadcast_to(mass, (4, LANES))


def last_kernel(me, own, one, two, three, total, rank_out, delta_out, masses, ordered):
    owned = total.shape[0]
    for r in range(4):
        part = slice(LANES * r, LANES * (r + 1))
        rank_out[:, part] = total[:, r, :]
        delta_out[:, part] = (
            own[0:owned, r, :] + one[0:owned, r, :] + two[0:owned, r, :] + three[0:owned, r, :]
        )
    for s, part in enumerate((own, one, two, three)):
        ordered[lax.rem(me[0] + 4 - s, 4)] = part[owned]
    masses[...] = (ordered[0] + ordered[1] + ordered[2] + ordered[3])[0:1]


def f32(*shape):
    return jax.ShapeDtypeStruct(shape, jnp.float32)


def s32(*shape):
    return jax.ShapeDtypeStruct(shape, jnp.int32)


def call(kernel, outs, specs_in, specs_out, scratch, vmem=4, cost=None):
    return pl.pallas_call(
        kernel,
        out_shape=outs,
        in_specs=specs_in,
        out_specs=specs_out,
        scratch_shapes=scratch,
        cost_estimate=cost,
        compiler_params=pltpu.CompilerParams(vmem_limit_bytes=vmem << 20),
    )


def on_device(rank_in, delta_in, out_degree, tile_weight, tile_source, tile_row, tile_valid):
    owned, width = delta_in.shape
    tiles = tile_row.shape[0]
    n_group = lax.axis_size(BLK)
    n_column = lax.axis_size("col")
    cells = owned * n_group * n_column * width
    me = lax.axis_index("col").astype(jnp.int32).reshape(1)
    asked = lax.all_to_all(
        tile_source.reshape(n_group, 1, 1), BLK, split_axis=0, concat_axis=0, tiled=True
    )
    held = f32(owned, 4, LANES)
    message = jax.ShapeDtypeStruct((n_group, 8, LANES), jnp.bfloat16)
    block_scratch = pltpu.VMEM((owned, 4, LANES), jnp.float32)
    table, scale, total, masses, contrib = call(
        functools.partial(stage_kernel, n_column),
        (s32(4 * tiles), held, held, f32(8, LANES), held),
        [SMEM] + [HBM] * 5,
        (SMEM,) + (VMEM,) * 4,
        [
            pltpu.VMEM((owned, width), jnp.float32),
            pltpu.VMEM((owned, width), jnp.float32),
            pltpu.VMEM((owned, width), jnp.int32),
            pltpu.SMEM((tiles,), jnp.int32),
            pltpu.SMEM((tiles,), jnp.int32),
            pltpu.SemaphoreType.DMA((5,)),
        ],
    )(me, *(pltpu.with_memory_space_constraint(x, pltpu.HBM) for x in (delta_in, rank_in, out_degree, tile_row, tile_valid)))
    out = call(
        first_kernel,
        message,
        [SMEM, VMEM],
        VMEM,
        [],
    )(asked, contrib)
    keep = functools.partial(pltpu.with_memory_space_constraint, memory_space=pltpu.VMEM)
    resident = pltpu.VMEM(tile_weight.shape, tile_weight.dtype)
    tile_scratch = [
        pltpu.VMEM((tiles, 8, LANES), jnp.float32),
        pltpu.VMEM((n_column * owned, 4, LANES), jnp.float32),
    ]
    for step in range(ITERS):
        picked = lax.all_to_all(out, BLK, split_axis=0, concat_axis=0, tiled=True)
        last = step == ITERS - 1
        marks = []
        if step == 0:
            *parts, weight, turned = call(
                functools.partial(start_tile_kernel, EARLY),
                (held,) * 4 + (resident,) * 2,
                [SMEM, VMEM, HBM],
                (VMEM,) * 6,
                tile_scratch + [pltpu.SemaphoreType.DMA((tiles,))],
            )(table, picked, pltpu.with_memory_space_constraint(tile_weight, pltpu.HBM))
            turned, mark = pl.pallas_call(
                functools.partial(turn_kernel, EARLY, tiles),
                out_shape=(resident, f32(8, LANES)),
                in_specs=[VMEM] * 3,
                out_specs=(VMEM, VMEM),
                input_output_aliases={2: 0},
                cost_estimate=pl.CostEstimate(flops=0, transcendentals=0, bytes_accessed=12 << 20),
                compiler_params=pltpu.CompilerParams(vmem_limit_bytes=4 << 20),
            )(keep(weight), parts[0], keep(turned))
            marks = [mark]
        else:
            parts = call(
                functools.partial(tile_kernel, last),
                (f32(owned + last, 4, LANES),) * 4,
                [SMEM, VMEM, VMEM],
                (VMEM,) * 4,
                tile_scratch,
            )(table, picked, keep(turned))
        own, others = parts[0], parts[1:]
        others = [
            lax.ppermute(part, "col", [(i, (i + s + 1) % n_column) for i in range(n_column)])
            for s, part in enumerate(others)
        ]
        if not last:
            out, total, masses = call(
                functools.partial(join_kernel, step + 1, cells),
                (message, held, f32(8, LANES)),
                [SMEM] + [VMEM] * (7 + len(marks)),
                (VMEM,) * 3,
                [block_scratch],
            )(asked, own, *others, scale, total, masses, *marks)
    rank_out, delta_out, stacked = call(
        last_kernel,
        (f32(owned, width), f32(owned, width), f32(1, LANES)),
        [SMEM] + [VMEM] * 5,
        (VMEM,) * 3,
        [pltpu.VMEM((4, 4, LANES), jnp.float32)],
    )(me, own, *others, total)
    return rank_out, delta_out, stacked[0, :ITERS]


def solution(mesh):
    finer = Mesh(
        mesh.devices.reshape(4, 4, 2, mesh.shape["col"]), ("blk_0", "blk_1", "blk_2", "col")
    )
    placed = (
        P(BLK_COL, None),
        P(BLK_COL, None),
        P(BLK_COL, None),
        P(BLK_COL, None, None),
        P(BLK_COL),
        P(BLK_COL),
        P(BLK_COL),
    )
    return jax.shard_map(
        on_device,
        mesh=finer,
        in_specs=placed,
        out_specs=(P(BLK_COL, None), P(BLK_COL, None), P()),
        check_vma=False,
    )
```

```python
import functools

import jax
import jax.numpy as jnp
from jax import lax
from jax.experimental import pallas as pl
from jax.experimental.pallas import tpu as pltpu
from jax.sharding import Mesh
from jax.sharding import PartitionSpec as P

ITERS = 6
BLK = ("blk_0", "blk_1", "blk_2")
BLK_COL = ("blk_0", "blk_1", "blk_2", "col")
LANES = 128
GROUP = 16
FIRST_GROUP = 4

damping = 0.85

VMEM = pl.BlockSpec(memory_space=pltpu.VMEM)
SMEM = pl.BlockSpec(memory_space=pltpu.SMEM)
HBM = pl.BlockSpec(memory_space=pltpu.HBM)


def lane_row(column):
    rows = lax.broadcasted_iota(jnp.int32, column.shape, 0)
    lanes = lax.broadcasted_iota(jnp.int32, column.shape, 1)
    return jnp.sum(jnp.where(rows == lanes, column, 0.0), axis=0, keepdims=True)


def pieces(value):
    high = value.astype(jnp.bfloat16).astype(jnp.float32)
    rest = value - high
    middle = rest.astype(jnp.bfloat16).astype(jnp.float32)
    low = (rest - middle).astype(jnp.bfloat16).astype(jnp.float32)
    return high, middle, low


def targets(cols, c, row, valid, table):
    tiles = row.shape[0]
    owned = tiles

    def target(i, carry):
        block = lax.rem(row[i] // owned + cols - c, cols) * owned + lax.rem(row[i], owned)
        table[i] = jnp.where(valid[i] != 0, block, cols * owned)
        return carry

    lax.fori_loop(0, tiles, target, 0)


def started(pairs, sems):
    copies = [pltpu.make_async_copy(*pair, sems.at[i]) for i, pair in enumerate(pairs)]
    for copy in copies:
        copy.start()
    return copies


def send(asked, contrib, message, extra):
    for b in range(message.shape[0]):
        block = contrib[asked[0, b]]
        if extra is None:
            message[b, 0:4, :] = block.astype(jnp.bfloat16)
        else:
            message[b] = jnp.concatenate([block, extra], axis=0).astype(jnp.bfloat16)


def first_kernel(source_hbm, delta_hbm, degree_hbm, message, source, delta, degree, contrib, sems):
    owned = delta.shape[0]
    for copy in started(((source_hbm, source), (delta_hbm, delta), (degree_hbm, degree)), sems):
        copy.wait()
    for r in range(4):
        part = slice(LANES * r, LANES * (r + 1))
        contrib[:, r, :] = delta[:, part] * (damping / degree[:, part].astype(jnp.float32))
    blocks = contrib[...].astype(jnp.bfloat16)
    for b in range(message.shape[0]):
        message[b, 0:owned] = blocks
        request = lax.rem(source[b], owned).astype(jnp.float32)
        message[b, owned] = jnp.full((4, LANES), request, jnp.float32).astype(jnp.bfloat16)


def window_kernel(cols, *refs):
    _, delta_hbm, rank_hbm, degree_hbm, row_hbm, valid_hbm = refs[:6]
    table, scale, total, masses = refs[6:10]
    delta_in, rank_in, degree, row, valid, sems = refs[10:]
    copies = started(
        (
            (row_hbm, row),
            (valid_hbm, valid),
            (delta_hbm, delta_in),
            (rank_hbm, rank_in),
            (degree_hbm, degree),
        ),
        sems,
    )

    for copy in copies:
        copy.wait()
    targets(cols, lax.axis_index("col"), row, valid, table)
    mass = jnp.zeros((1, LANES), jnp.float32)
    for r in range(4):
        part = slice(LANES * r, LANES * (r + 1))
        delta = delta_in[:, part]
        scale[:, r, :] = damping / degree[:, part].astype(jnp.float32)
        total[:, r, :] = rank_in[:, part] + delta
        mass = mass + jnp.sum(jnp.abs(delta), axis=0, keepdims=True)
    masses[...] = jnp.concatenate([mass, jnp.zeros((7, LANES), jnp.float32)], axis=0)


def join_kernel(step, cells, asked, own, one, two, three, scale, total, masses, *rest):
    message, total_out, masses_out, contrib = rest
    delta = own[...] + one[...] + two[...] + three[...]
    total_out[...] = total[...] + delta
    contrib[...] = delta * scale[...]
    mass = jnp.sum(jnp.sum(jnp.abs(delta), axis=0), axis=0, keepdims=True)
    rows = lax.broadcasted_iota(jnp.int32, (8, LANES), 0)
    merged = jnp.where(rows == step, mass, masses[...])
    masses_out[...] = merged
    extra = None
    if step == ITERS - 1:
        sums = jnp.broadcast_to(jnp.sum(merged, axis=1, keepdims=True) / cells, (8, LANES))
        extra = jnp.concatenate([*pieces(lane_row(sums)), jnp.zeros((1, LANES), jnp.float32)], axis=0)
    send(asked, contrib, message, extra)


def product(vectors, rows, j, first, weight, contracted):
    wide = jnp.concatenate(
        [jnp.broadcast_to(vectors[j, first + r][None], (8, LANES)) for r in range(4)], axis=1
    )
    found = lax.dot_general(
        wide.astype(jnp.bfloat16),
        weight,
        (((1,), (contracted,)), ((), ())),
        preferred_element_type=jnp.float32,
    )
    block = found[:, 3 * LANES :]
    for r in (2, 1, 0):
        block = jnp.where(rows == r, found[:, LANES * r : LANES * (r + 1)], block)
    return block[:4]


def start_tile_kernel(cols, *refs):
    source_hbm, row_hbm, valid_hbm, received, weight = refs[:5]
    own, one, two, three, turned, asked = refs[5:11]
    source, row, valid, table, vectors, sums, small_sems = refs[11:]
    tiles = weight.shape[0]
    owned = tiles

    copies = started(((source_hbm, source), (row_hbm, row), (valid_hbm, valid)), small_sems)
    sums[...] = jnp.zeros_like(sums)
    asking = lax.broadcasted_iota(jnp.int32, (tiles, LANES), 0)
    lanes = lax.broadcasted_iota(jnp.int32, (tiles, LANES), 1)
    requests = received[:, owned, :, :].astype(jnp.float32)[:, 0, :]
    asked[...] = jnp.sum(
        jnp.where(asking == lanes, requests, 0.0), axis=0, keepdims=True
    ).astype(jnp.int32)
    for copy in copies:
        copy.wait()
    targets(cols, lax.axis_index("col"), row, valid, table)
    for j in range(tiles):
        vectors[j, 0:4] = received[j, lax.rem(source[j], owned)].astype(jnp.float32)
    rows = lax.broadcasted_iota(jnp.int32, (8, LANES), 0)

    def group(g, carry):
        found = []
        for u in range(FIRST_GROUP):
            j = g * FIRST_GROUP + u
            tile = weight[j]
            turned[j] = tile.T
            found.append((j, product(vectors, rows, j, 0, tile, 1)))
        for j, block in found:
            q = table[j]
            sums[q] = sums[q] + block
        return carry

    lax.fori_loop(0, tiles // FIRST_GROUP, group, 0)
    for s, out in enumerate((own, one, two, three)):
        out[...] = sums[s * owned : (s + 1) * owned]


def tile_kernel(last, table, picked, turned, own, one, two, three, vectors, sums):
    owned = tiles = picked.shape[0]
    sums[...] = jnp.zeros_like(sums)
    vectors[...] = picked[...].astype(jnp.float32)
    rows = lax.broadcasted_iota(jnp.int32, (8, LANES), 0)

    def group(g, carry):
        found = []
        for u in range(GROUP):
            j = g * GROUP + u
            found.append((j, product(vectors, rows, j, 0, turned[j], 0)))
        for j, block in found:
            q = table[j]
            sums[q] = sums[q] + block
        return carry

    lax.fori_loop(0, tiles // GROUP, group, 0)
    for s, out in enumerate((own, one, two, three)):
        out[0:owned] = sums[s * owned : (s + 1) * owned]
    if last:
        mass = jnp.zeros((1, LANES), jnp.float32)
        for r in (4, 5, 6):
            mass = mass + jnp.sum(vectors[:, r, :], axis=0, keepdims=True)
        for out in (own, one, two, three):
            out[owned] = jnp.broadcast_to(mass, (4, LANES))


def last_kernel(own, one, two, three, total, rank_out, delta_out, masses, ordered):
    owned = total.shape[0]
    for r in range(4):
        part = slice(LANES * r, LANES * (r + 1))
        rank_out[:, part] = total[:, r, :]
        delta_out[:, part] = (
            own[0:owned, r, :] + one[0:owned, r, :] + two[0:owned, r, :] + three[0:owned, r, :]
        )
    for s, part in enumerate((own, one, two, three)):
        ordered[lax.rem(lax.axis_index("col") + 4 - s, 4)] = part[owned]
    mass = ordered[0] + ordered[1] + ordered[2] + ordered[3]
    masses[...] = mass[0:1, 0 : masses.shape[1]]


def f32(*shape):
    return jax.ShapeDtypeStruct(shape, jnp.float32)


def s32(*shape):
    return jax.ShapeDtypeStruct(shape, jnp.int32)


def call(kernel, outs, specs_in, specs_out, scratch, vmem=4, cost=None):
    return pl.pallas_call(
        kernel,
        out_shape=outs,
        in_specs=specs_in,
        out_specs=specs_out,
        scratch_shapes=scratch,
        cost_estimate=cost,
        compiler_params=pltpu.CompilerParams(vmem_limit_bytes=vmem << 20),
    )


def on_device(rank_in, delta_in, out_degree, tile_weight, tile_source, tile_row, tile_valid):
    owned, width = delta_in.shape
    tiles = tile_row.shape[0]
    n_group = lax.axis_size(BLK)
    n_column = lax.axis_size("col")
    cells = owned * n_group * n_column * width
    held = f32(owned, 4, LANES)
    message = jax.ShapeDtypeStruct((n_group, 8, LANES), jnp.bfloat16)
    block_scratch = pltpu.VMEM((owned, 4, LANES), jnp.float32)
    keep = functools.partial(pltpu.with_memory_space_constraint, memory_space=pltpu.VMEM)
    leave = functools.partial(pltpu.with_memory_space_constraint, memory_space=pltpu.HBM)
    resident = pltpu.VMEM(tile_weight.shape, tile_weight.dtype)
    indices = pltpu.SMEM((tiles,), jnp.int32)
    floats = pltpu.VMEM((owned, width), jnp.float32)
    integers = pltpu.VMEM((owned, width), jnp.int32)
    tile_scratch = [
        pltpu.VMEM((tiles, 8, LANES), jnp.float32),
        pltpu.VMEM((n_column * owned + 1, 4, LANES), jnp.float32),
    ]
    out = call(
        first_kernel,
        jax.ShapeDtypeStruct((n_group, owned + 1, 4, LANES), jnp.bfloat16),
        [HBM] * 3,
        VMEM,
        [indices, floats, integers, block_scratch, pltpu.SemaphoreType.DMA((3,))],
        cost=pl.CostEstimate(flops=40 << 30, transcendentals=0, bytes_accessed=128 << 20),
    )(leave(tile_source), leave(delta_in), leave(out_degree))
    for step in range(ITERS):
        picked = lax.all_to_all(out, BLK, split_axis=0, concat_axis=0, tiled=True)
        last = step == ITERS - 1
        if step == 0:
            *parts, turned, asked = call(
                functools.partial(start_tile_kernel, n_column),
                (held,) * 4 + (resident, s32(1, LANES)),
                [HBM] * 3 + [VMEM, VMEM],
                (VMEM,) * 6,
                [indices] * 4
                + tile_scratch
                + [pltpu.SemaphoreType.DMA((3,))],
            )(
                leave(tile_source),
                leave(tile_row),
                leave(tile_valid),
                picked,
                tile_weight,
            )
            table, scale, total, masses = call(
                functools.partial(window_kernel, n_column),
                (s32(tiles), held, held, f32(8, LANES)),
                [VMEM] + [HBM] * 5,
                (SMEM,) + (VMEM,) * 3,
                [floats, floats, integers, indices, indices, pltpu.SemaphoreType.DMA((5,))],
                cost=pl.CostEstimate(flops=0, transcendentals=0, bytes_accessed=8 << 20),
            )(
                parts[0],
                leave(delta_in),
                leave(rank_in),
                leave(out_degree),
                leave(tile_row),
                leave(tile_valid),
            )
        else:
            parts = call(
                functools.partial(tile_kernel, last),
                (f32(owned + last, 4, LANES),) * 4,
                [SMEM, VMEM, VMEM],
                (VMEM,) * 4,
                tile_scratch,
            )(table, picked, keep(turned))
        own, others = parts[0], parts[1:]
        others = [
            lax.ppermute(part, "col", [(i, (i + s + 1) % n_column) for i in range(n_column)])
            for s, part in enumerate(others)
        ]
        if not last:
            out, total, masses = call(
                functools.partial(join_kernel, step + 1, cells),
                (message, held, f32(8, LANES)),
                [SMEM] + [VMEM] * 7,
                (VMEM,) * 3,
                [block_scratch],
            )(asked, own, *others, scale, total, masses)
    rank_out, delta_out, stacked = call(
        last_kernel,
        (f32(owned, width), f32(owned, width), f32(1, ITERS)),
        [VMEM] * 5,
        (VMEM,) * 3,
        [pltpu.VMEM((4, 4, LANES), jnp.float32)],
    )(own, *others, total)
    return rank_out, delta_out, stacked.reshape(ITERS)


def solution(mesh):
    finer = Mesh(
        mesh.devices.reshape(4, 4, 2, mesh.shape["col"]), ("blk_0", "blk_1", "blk_2", "col")
    )
    placed = (
        P(BLK_COL, None),
        P(BLK_COL, None),
        P(BLK_COL, None),
        P(BLK_COL, None, None),
        P(BLK_COL),
        P(BLK_COL),
        P(BLK_COL),
    )
    return jax.shard_map(
        on_device,
        mesh=finer,
        in_specs=placed,
        out_specs=(P(BLK_COL, None), P(BLK_COL, None), P()),
        check_vma=False,
    )
```

```python
import functools

import jax
import jax.numpy as jnp
from jax import lax
from jax.experimental import pallas as pl
from jax.experimental.pallas import tpu as pltpu
from jax.sharding import Mesh
from jax.sharding import PartitionSpec as P

ITERS = 6
BLK = ("blk_0", "blk_1", "blk_2")
BLK_COL = ("blk_0", "blk_1", "blk_2", "col")
LANES = 128
GROUP = 32
FIRST_GROUP = 4

damping = 0.85

VMEM = pl.BlockSpec(memory_space=pltpu.VMEM)
SMEM = pl.BlockSpec(memory_space=pltpu.SMEM)
HBM = pl.BlockSpec(memory_space=pltpu.HBM)


def lane_row(column):
    rows = lax.broadcasted_iota(jnp.int32, column.shape, 0)
    lanes = lax.broadcasted_iota(jnp.int32, column.shape, 1)
    return jnp.sum(jnp.where(rows == lanes, column, 0.0), axis=0, keepdims=True)


def pieces(value):
    high = value.astype(jnp.bfloat16).astype(jnp.float32)
    rest = value - high
    middle = rest.astype(jnp.bfloat16).astype(jnp.float32)
    low = (rest - middle).astype(jnp.bfloat16).astype(jnp.float32)
    return high, middle, low


def targets(cols, c, row, valid, table):
    tiles = row.shape[0]
    owned = tiles

    def target(i, carry):
        block = lax.rem(row[i] // owned + cols - c, cols) * owned + lax.rem(row[i], owned)
        table[i] = jnp.where(valid[i] != 0, block, cols * owned)
        return carry

    lax.fori_loop(0, tiles, target, 0)


def started(pairs, sems):
    copies = [pltpu.make_async_copy(*pair, sems.at[i]) for i, pair in enumerate(pairs)]
    for copy in copies:
        copy.start()
    return copies


def first_kernel(source_hbm, delta_hbm, degree_hbm, message, source, delta, degree, contrib, sems):
    owned = delta.shape[0]
    for copy in started(((source_hbm, source), (delta_hbm, delta), (degree_hbm, degree)), sems):
        copy.wait()
    for r in range(4):
        part = slice(LANES * r, LANES * (r + 1))
        contrib[:, r, :] = delta[:, part] * (damping / degree[:, part].astype(jnp.float32))
    blocks = contrib[...].astype(jnp.bfloat16)
    for b in range(message.shape[0]):
        message[b, 0:owned] = blocks
        request = lax.rem(source[b], owned).astype(jnp.float32)
        message[b, owned] = jnp.full((4, LANES), request, jnp.float32).astype(jnp.bfloat16)


def window_kernel(cols, *refs):
    _, delta_hbm, rank_hbm, degree_hbm, row_hbm, valid_hbm = refs[:6]
    table, degrees, total, masses = refs[6:10]
    delta_in, rank_in, degree, row, valid, sems = refs[10:]
    copies = started(
        (
            (row_hbm, row),
            (valid_hbm, valid),
            (delta_hbm, delta_in),
            (rank_hbm, rank_in),
            (degree_hbm, degree),
        ),
        sems,
    )

    for copy in copies:
        copy.wait()
    targets(cols, lax.axis_index("col"), row, valid, table)
    mass = jnp.zeros((1, LANES), jnp.float32)
    for r in range(4):
        part = slice(LANES * r, LANES * (r + 1))
        delta = delta_in[:, part]
        degrees[:, r, :] = degree[:, part].astype(jnp.float32)
        total[:, r, :] = rank_in[:, part] + delta
        mass = mass + jnp.sum(jnp.abs(delta), axis=0, keepdims=True)
    masses[...] = jnp.concatenate([mass, jnp.zeros((7, LANES), jnp.float32)], axis=0)


def one_join_kernel(cols, own, one, two, three, degrees, total, masses, *refs):
    message, total_out, masses_out, wants, contrib, asked, sem = refs
    owned = total.shape[0]
    parts = (own, one, two, three)
    for s, part in enumerate(parts):
        at = (cols - s) % cols
        wants[at : at + 1, :] = part[owned, 0:1, :].astype(jnp.int32) + at * owned
    copy = pltpu.make_async_copy(wants, asked, sem)
    copy.start()
    delta = own[0:owned] + one[0:owned] + two[0:owned] + three[0:owned]
    total_out[...] = total[...] + delta
    contrib[:, 0:4, :] = delta * (damping / degrees[...])
    contrib[:, 4:8, :] = degrees[...]
    mass = jnp.sum(jnp.sum(jnp.abs(delta), axis=0), axis=0, keepdims=True)
    rows = lax.broadcasted_iota(jnp.int32, (8, LANES), 0)
    masses_out[...] = jnp.where(rows == 1, mass, masses[...])
    copy.wait()
    for b in range(message.shape[0]):
        message[b] = contrib[asked[0, b]].astype(jnp.bfloat16)


def tally(steps, own, one, two, three, total, masses):
    owned = total.shape[0]
    ranks = total[...]
    merged = masses[...]
    rows = lax.broadcasted_iota(jnp.int32, (8, LANES), 0)
    for t, step in enumerate(steps):
        part = slice(t * owned, (t + 1) * owned)
        delta = own[part] + one[part] + two[part] + three[part]
        ranks = ranks + delta
        mass = jnp.sum(jnp.sum(jnp.abs(delta), axis=0), axis=0, keepdims=True)
        merged = jnp.where(rows == step, mass, merged)
    return ranks, merged, delta


def early_join_kernel(steps, _, own, one, two, three, total, masses, total_out, masses_out):
    total_out[...], masses_out[...], _ = tally(steps, own, one, two, three, total, masses)


def late_join_kernel(cells, wants, own, one, two, three, degrees, total, masses, *refs):
    message, total_out, contrib = refs
    total_out[...], merged, delta = tally((ITERS - 1,), own, one, two, three, total, masses)
    contrib[...] = delta * (damping / degrees[...])
    sums = jnp.broadcast_to(jnp.sum(merged, axis=1, keepdims=True) / cells, (8, LANES))
    extra = jnp.concatenate([*pieces(lane_row(sums)), jnp.zeros((1, LANES), jnp.float32)], axis=0)
    for b in range(message.shape[0]):
        message[b] = jnp.concatenate([contrib[wants[0, b]], extra], axis=0).astype(jnp.bfloat16)


def product(vectors, rows, j, first, weight, contracted):
    wide = jnp.concatenate(
        [jnp.broadcast_to(vectors[j, first + r][None], (8, LANES)) for r in range(4)], axis=1
    )
    found = lax.dot_general(
        wide.astype(jnp.bfloat16),
        weight,
        (((1,), (contracted,)), ((), ())),
        preferred_element_type=jnp.float32,
    )
    block = found[:, 3 * LANES :]
    for r in (2, 1, 0):
        block = jnp.where(rows == r, found[:, LANES * r : LANES * (r + 1)], block)
    return block[:4]


def start_tile_kernel(cols, *refs):
    source_hbm, row_hbm, valid_hbm, received, weight = refs[:5]
    own, one, two, three, turned = refs[5:10]
    source, row, valid, table, vectors, sums, small_sems = refs[10:]
    tiles = weight.shape[0]
    owned = tiles

    copies = started(((source_hbm, source), (row_hbm, row), (valid_hbm, valid)), small_sems)
    sums[...] = jnp.zeros_like(sums)
    asking = lax.broadcasted_iota(jnp.int32, (tiles, LANES), 0)
    lanes = lax.broadcasted_iota(jnp.int32, (tiles, LANES), 1)
    requests = received[:, owned, :, :].astype(jnp.float32)[:, 0, :]
    asked = jnp.sum(jnp.where(asking == lanes, requests, 0.0), axis=0, keepdims=True)
    for out in (own, one, two, three):
        out[owned] = jnp.broadcast_to(asked, (4, LANES))
    for copy in copies:
        copy.wait()
    targets(cols, lax.axis_index("col"), row, valid, table)
    for j in range(tiles):
        vectors[j, 0:4] = received[j, lax.rem(source[j], owned)].astype(jnp.float32)
    rows = lax.broadcasted_iota(jnp.int32, (8, LANES), 0)

    def group(g, carry):
        found = []
        for u in range(FIRST_GROUP):
            j = g * FIRST_GROUP + u
            tile = weight[j]
            turned[j] = tile.T
            found.append((j, product(vectors, rows, j, 0, tile, 1)))
        for j, block in found:
            q = table[j]
            sums[q] = sums[q] + block
        return carry

    lax.fori_loop(0, tiles // FIRST_GROUP, group, 0)
    for s, out in enumerate((own, one, two, three)):
        out[0:owned] = sums[s * owned : (s + 1) * owned]


def multiply(table, vectors, turned, sums):
    tiles = turned.shape[0]
    sums[...] = jnp.zeros_like(sums)
    rows = lax.broadcasted_iota(jnp.int32, (8, LANES), 0)

    def group(g, carry):
        found = []
        for u in range(GROUP):
            j = g * GROUP + u
            found.append((j, product(vectors, rows, j, 0, turned[j], 0)))
        for j, block in found:
            q = table[j]
            sums[q] = sums[q] + block
        return carry

    lax.fori_loop(0, tiles // GROUP, group, 0)


def take_sums(arrived, scale, vectors):
    tiles = vectors.shape[0]
    columns = arrived.shape[0] // tiles
    blocks = jnp.sum(arrived[...].reshape(tiles, columns, 4, LANES), axis=1)
    vectors[:, 0:4, :] = blocks * scale[...]


def give_parts(outs, earlier, sums, owned):
    for s, out in enumerate(outs):
        before = earlier[s :: len(outs)]
        for t, part in enumerate(before):
            out[t * owned : (t + 1) * owned] = part[...]
        out[len(before) * owned :] = sums[s * owned : (s + 1) * owned]


def relay_kernel(cols, first, *refs):
    table, wants, arrived, *refs, vectors, sums = refs
    owned = vectors.shape[0]
    if first:
        turned, message, *parts, scale = refs
        vectors[...] = arrived[...].astype(jnp.float32)
        scale[...] = damping / vectors[:, 4:8, :]
        earlier = ()
    else:
        scale, turned, *earlier, message = refs[:-cols]
        parts = refs[-cols:]
        take_sums(arrived, scale, vectors)
    multiply(table, vectors, turned, sums)
    c = lax.axis_index("col")
    for s in range(cols):
        to = lax.rem(c + s, cols)
        for b in range(message.shape[0] // cols):
            message[b * cols + to] = sums[wants[s, b]]
    give_parts(parts, earlier, sums, owned)


def collect_kernel(table, arrived, scale, turned, own, one, two, three, vectors, sums):
    take_sums(arrived, scale, vectors)
    multiply(table, vectors, turned, sums)
    give_parts((own, one, two, three), (), sums, vectors.shape[0])


def end_tile_kernel(table, picked, turned, own, one, two, three, vectors, sums):
    owned = picked.shape[0]
    vectors[...] = picked[...].astype(jnp.float32)
    multiply(table, vectors, turned, sums)
    mass = jnp.zeros((1, LANES), jnp.float32)
    for r in (4, 5, 6):
        mass = mass + jnp.sum(vectors[:, r, :], axis=0, keepdims=True)
    for s, out in enumerate((own, one, two, three)):
        out[0:owned] = sums[s * owned : (s + 1) * owned]
        out[owned] = jnp.broadcast_to(mass, (4, LANES))


def last_kernel(own, one, two, three, total, rank_out, delta_out, masses, ordered):
    owned = total.shape[0]
    for r in range(4):
        part = slice(LANES * r, LANES * (r + 1))
        rank_out[:, part] = total[:, r, :]
        delta_out[:, part] = (
            own[0:owned, r, :] + one[0:owned, r, :] + two[0:owned, r, :] + three[0:owned, r, :]
        )
    for s, part in enumerate((own, one, two, three)):
        ordered[lax.rem(lax.axis_index("col") + 4 - s, 4)] = part[owned]
    mass = ordered[0] + ordered[1] + ordered[2] + ordered[3]
    masses[...] = mass[0:1, 0 : masses.shape[1]]


def f32(*shape):
    return jax.ShapeDtypeStruct(shape, jnp.float32)


def s32(*shape):
    return jax.ShapeDtypeStruct(shape, jnp.int32)


def call(kernel, outs, specs_in, specs_out, scratch, vmem=4, cost=None):
    return pl.pallas_call(
        kernel,
        out_shape=outs,
        in_specs=specs_in,
        out_specs=specs_out,
        scratch_shapes=scratch,
        cost_estimate=cost,
        compiler_params=pltpu.CompilerParams(vmem_limit_bytes=vmem << 20),
    )


def on_device(rank_in, delta_in, out_degree, tile_weight, tile_source, tile_row, tile_valid):
    owned, width = delta_in.shape
    tiles = tile_row.shape[0]
    n_group = lax.axis_size(BLK)
    n_column = lax.axis_size("col")
    cells = owned * n_group * n_column * width
    held = f32(owned, 4, LANES)
    message = jax.ShapeDtypeStruct((n_group, 8, LANES), jnp.bfloat16)
    block_scratch = pltpu.VMEM((owned, 4, LANES), jnp.float32)
    keep = functools.partial(pltpu.with_memory_space_constraint, memory_space=pltpu.VMEM)
    leave = functools.partial(pltpu.with_memory_space_constraint, memory_space=pltpu.HBM)
    resident = pltpu.VMEM(tile_weight.shape, tile_weight.dtype)
    indices = pltpu.SMEM((tiles,), jnp.int32)
    floats = pltpu.VMEM((owned, width), jnp.float32)
    integers = pltpu.VMEM((owned, width), jnp.int32)
    tile_scratch = [
        pltpu.VMEM((tiles, 8, LANES), jnp.float32),
        pltpu.VMEM((n_column * owned + 1, 4, LANES), jnp.float32),
    ]
    out = call(
        first_kernel,
        jax.ShapeDtypeStruct((n_group, owned + 1, 4, LANES), jnp.bfloat16),
        [HBM] * 3,
        VMEM,
        [indices, floats, integers, block_scratch, pltpu.SemaphoreType.DMA((3,))],
        cost=pl.CostEstimate(flops=40 << 30, transcendentals=0, bytes_accessed=128 << 20),
    )(leave(tile_source), leave(delta_in), leave(out_degree))
    def over_columns(parts):
        return [parts[0]] + [
            lax.ppermute(
                parts[s], "col", [(i, (i + s) % n_column) for i in range(n_column)]
            )
            for s in range(1, n_column)
        ]

    def to_groups(message):
        return lax.all_to_all(message, BLK, split_axis=0, concat_axis=0, tiled=True)

    longer = f32(owned + 1, 4, LANES)
    received = to_groups(out)
    *parts, turned = call(
        functools.partial(start_tile_kernel, n_column),
        (longer,) * 4 + (resident,),
        [HBM] * 3 + [VMEM, VMEM],
        (VMEM,) * 5,
        [indices] * 4 + tile_scratch + [pltpu.SemaphoreType.DMA((3,))],
    )(leave(tile_source), leave(tile_row), leave(tile_valid), received, tile_weight)
    turned = keep(turned)
    table, degrees, total, masses = call(
        functools.partial(window_kernel, n_column),
        (s32(tiles), held, held, f32(8, LANES)),
        [VMEM] + [HBM] * 5,
        (SMEM,) + (VMEM,) * 3,
        [floats, floats, integers, indices, indices, pltpu.SemaphoreType.DMA((5,))],
        cost=pl.CostEstimate(flops=0, transcendentals=0, bytes_accessed=8 << 20),
    )(
        parts[0],
        leave(delta_in),
        leave(rank_in),
        leave(out_degree),
        leave(tile_row),
        leave(tile_valid),
    )
    out, total, masses, wants = call(
        functools.partial(one_join_kernel, n_column),
        (message, held, f32(8, LANES), s32(8, LANES)),
        [VMEM] * 7,
        (VMEM,) * 4,
        [
            pltpu.VMEM((owned, 8, LANES), jnp.float32),
            pltpu.SMEM((8, LANES), jnp.int32),
            pltpu.SemaphoreType.DMA(()),
        ],
    )(*over_columns(parts), degrees, total, masses)
    arrived = to_groups(out)
    relayed = f32(n_group * n_column, 4, LANES)
    relays = range(2, ITERS - 1)
    earlier = []
    for step in relays:
        first, final = step == relays[0], step == relays[-1]
        given = (table, wants, arrived) + (() if first else (scale,)) + (turned,)
        given += tuple(earlier) if final else ()
        rows = len(relays) * owned if final else owned
        out, *parts = call(
            functools.partial(relay_kernel, n_column, first),
            (relayed,) + (f32(rows, 4, LANES),) * 4 + (held,) * first,
            [SMEM, SMEM] + [VMEM] * (len(given) - 2),
            (VMEM,) * (5 + first),
            tile_scratch,
        )(*given)
        if first:
            scale = parts.pop()
        earlier += parts
        arrived = lax.all_to_all(out, BLK_COL, split_axis=0, concat_axis=0, tiled=True)
    middle = over_columns(parts)
    parts = call(
        collect_kernel,
        (held,) * 4,
        [SMEM] + [VMEM] * 3,
        (VMEM,) * 4,
        tile_scratch,
    )(table, arrived, scale, turned)
    total, masses = call(
        functools.partial(early_join_kernel, tuple(relays)),
        (held, f32(8, LANES)),
        [VMEM] * 7,
        (VMEM,) * 2,
        [],
        cost=pl.CostEstimate(flops=0, transcendentals=0, bytes_accessed=8 << 20),
    )(parts[0], *middle, total, masses)
    out, total = call(
        functools.partial(late_join_kernel, cells),
        (message, held),
        [SMEM] + [VMEM] * 7,
        (VMEM,) * 2,
        [block_scratch],
    )(wants, *over_columns(parts), degrees, total, masses)
    parts = call(
        end_tile_kernel,
        (longer,) * 4,
        [SMEM, VMEM, VMEM],
        (VMEM,) * 4,
        tile_scratch,
    )(table, to_groups(out), turned)
    rank_out, delta_out, stacked = call(
        last_kernel,
        (f32(owned, width), f32(owned, width), f32(1, ITERS)),
        [VMEM] * 5,
        (VMEM,) * 3,
        [pltpu.VMEM((4, 4, LANES), jnp.float32)],
    )(*over_columns(parts), total)
    return rank_out, delta_out, stacked.reshape(ITERS)


def solution(mesh):
    finer = Mesh(
        mesh.devices.reshape(4, 4, 2, mesh.shape["col"]), ("blk_0", "blk_1", "blk_2", "col")
    )
    placed = (
        P(BLK_COL, None),
        P(BLK_COL, None),
        P(BLK_COL, None),
        P(BLK_COL, None, None),
        P(BLK_COL),
        P(BLK_COL),
        P(BLK_COL),
    )
    return jax.shard_map(
        on_device,
        mesh=finer,
        in_specs=placed,
        out_specs=(P(BLK_COL, None), P(BLK_COL, None), P()),
        check_vma=False,
    )
```

```python
import functools

import jax
import jax.numpy as jnp
from jax import lax
from jax.experimental import pallas as pl
from jax.experimental.pallas import tpu as pltpu
from jax.sharding import Mesh
from jax.sharding import PartitionSpec as P

ITERS = 6
BLK = ("blk_0", "blk_1", "blk_2")
BLK_COL = ("blk_0", "blk_1", "blk_2", "col")
LANES = 128
CORES = 2
GROUP = 32
FIRST_GROUP = 16

damping = 0.85

VMEM = pl.BlockSpec(memory_space=pltpu.VMEM)
SMEM = pl.BlockSpec(memory_space=pltpu.SMEM)
HBM = pl.BlockSpec(memory_space=pltpu.HBM)


def lane_row(column):
    rows = lax.broadcasted_iota(jnp.int32, column.shape, 0)
    lanes = lax.broadcasted_iota(jnp.int32, column.shape, 1)
    return jnp.sum(jnp.where(rows == lanes, column, 0.0), axis=0, keepdims=True)


def pieces(value):
    high = value.astype(jnp.bfloat16).astype(jnp.float32)
    rest = value - high
    middle = rest.astype(jnp.bfloat16).astype(jnp.float32)
    low = (rest - middle).astype(jnp.bfloat16).astype(jnp.float32)
    return high, middle, low


def targets(cols, c, row, valid, table):
    tiles = row.shape[0]
    owned = tiles

    def target(i, carry):
        block = lax.rem(row[i] // owned + cols - c, cols) * owned + lax.rem(row[i], owned)
        table[i] = jnp.where(valid[i] != 0, block, cols * owned)
        return carry

    lax.fori_loop(0, tiles, target, 0)


def started(pairs, sems):
    copies = [pltpu.make_async_copy(*pair, sems.at[i]) for i, pair in enumerate(pairs)]
    for copy in copies:
        copy.start()
    return copies


def first_kernel(source_hbm, delta_hbm, degree_hbm, message, source, delta, degree, contrib, sems):
    owned = delta.shape[0]
    for copy in started(((source_hbm, source), (delta_hbm, delta), (degree_hbm, degree)), sems):
        copy.wait()
    for r in range(4):
        part = slice(LANES * r, LANES * (r + 1))
        contrib[:, r, :] = delta[:, part] * (damping / degree[:, part].astype(jnp.float32))
    half = owned // CORES
    blocks = contrib[...].astype(jnp.bfloat16)
    for b in range(message.shape[0]):
        core = b % CORES
        message[b, 0:half] = blocks[core * half : (core + 1) * half]
        request = lax.rem(source[b], owned).astype(jnp.float32)
        message[b, half] = jnp.full((4, LANES), request, jnp.float32).astype(jnp.bfloat16)


def window_kernel(cols, *refs):
    _, delta_hbm, rank_hbm, degree_hbm, row_hbm, valid_hbm = refs[:6]
    table, degrees, total, masses = refs[6:10]
    delta_in, rank_in, degree, row, valid, sems = refs[10:]
    copies = started(
        (
            (row_hbm, row),
            (valid_hbm, valid),
            (delta_hbm, delta_in),
            (rank_hbm, rank_in),
            (degree_hbm, degree),
        ),
        sems,
    )

    for copy in copies:
        copy.wait()
    targets(cols, lax.axis_index("col"), row, valid, table)
    mass = jnp.zeros((1, LANES), jnp.float32)
    for r in range(4):
        part = slice(LANES * r, LANES * (r + 1))
        delta = delta_in[:, part]
        degrees[:, r, :] = degree[:, part].astype(jnp.float32)
        total[:, r, :] = rank_in[:, part] + delta
        mass = mass + jnp.sum(jnp.abs(delta), axis=0, keepdims=True)
    masses[...] = jnp.concatenate([mass, jnp.zeros((7, LANES), jnp.float32)], axis=0)


def one_join_kernel(cols, own, one, two, three, degrees, total, masses, *refs):
    message, total_out, masses_out, wants, contrib, asked, sem = refs
    owned = total.shape[0]
    parts = (own, one, two, three)
    for s, part in enumerate(parts):
        at = (cols - s) % cols
        wants[at : at + 1, :] = part[owned, 0:1, :].astype(jnp.int32) + at * owned
    copy = pltpu.make_async_copy(wants, asked, sem)
    copy.start()
    delta = own[0:owned] + one[0:owned] + two[0:owned] + three[0:owned]
    total_out[...] = total[...] + delta
    contrib[:, 0:4, :] = delta * (damping / degrees[...])
    contrib[:, 4:8, :] = degrees[...]
    mass = jnp.sum(jnp.sum(jnp.abs(delta), axis=0), axis=0, keepdims=True)
    rows = lax.broadcasted_iota(jnp.int32, (8, LANES), 0)
    masses_out[...] = jnp.where(rows == 1, mass, masses[...])
    copy.wait()
    for b in range(message.shape[0]):
        message[b] = contrib[asked[0, b]].astype(jnp.bfloat16)


def tally(steps, own, one, two, three, total, masses):
    owned = total.shape[0]
    ranks = total[...]
    merged = masses[...]
    rows = lax.broadcasted_iota(jnp.int32, (8, LANES), 0)
    for t, step in enumerate(steps):
        part = slice(t * owned, (t + 1) * owned)
        delta = own[part] + one[part] + two[part] + three[part]
        ranks = ranks + delta
        mass = jnp.sum(jnp.sum(jnp.abs(delta), axis=0), axis=0, keepdims=True)
        merged = jnp.where(rows == step, mass, merged)
    return ranks, merged, delta


def early_join_kernel(steps, _, own, one, two, three, total, masses, total_out, masses_out):
    total_out[...], masses_out[...], _ = tally(steps, own, one, two, three, total, masses)


def late_join_kernel(cells, wants, own, one, two, three, degrees, total, masses, *refs):
    message, total_out, contrib = refs
    total_out[...], merged, delta = tally((ITERS - 1,), own, one, two, three, total, masses)
    contrib[...] = delta * (damping / degrees[...])
    sums = jnp.broadcast_to(jnp.sum(merged, axis=1, keepdims=True) / cells, (8, LANES))
    extra = jnp.concatenate([*pieces(lane_row(sums)), jnp.zeros((1, LANES), jnp.float32)], axis=0)
    for b in range(message.shape[0]):
        message[b] = jnp.concatenate([contrib[wants[0, b]], extra], axis=0).astype(jnp.bfloat16)


def product(vectors, rows, j, first, weight, contracted):
    wide = jnp.concatenate(
        [jnp.broadcast_to(vectors[j, first + r][None], (8, LANES)) for r in range(4)], axis=1
    )
    found = lax.dot_general(
        wide.astype(jnp.bfloat16),
        weight,
        (((1,), (contracted,)), ((), ())),
        preferred_element_type=jnp.float32,
    )
    block = found[:, 3 * LANES :]
    for r in (2, 1, 0):
        block = jnp.where(rows == r, found[:, LANES * r : LANES * (r + 1)], block)
    return block[:4]


def start_tile_kernel(cols, *refs):
    source_hbm, row_hbm, valid_hbm, received, swapped, weight = refs[:6]
    own, one, two, three, turned = refs[6:11]
    source, row, valid, table, vectors, sums, small_sems = refs[11:]
    tiles = weight.shape[0]
    owned = tiles

    copies = started(((source_hbm, source), (row_hbm, row), (valid_hbm, valid)), small_sems)
    sums[...] = jnp.zeros_like(sums)
    asking = lax.broadcasted_iota(jnp.int32, (tiles, LANES), 0)
    lanes = lax.broadcasted_iota(jnp.int32, (tiles, LANES), 1)
    half = owned // CORES
    requests = received[:, half, :, :].astype(jnp.float32)[:, 0, :]
    asked = jnp.sum(jnp.where(asking == lanes, requests, 0.0), axis=0, keepdims=True)
    for out in (own, one, two, three):
        out[owned] = jnp.broadcast_to(asked, (4, LANES))
    for copy in copies:
        copy.wait()
    targets(cols, lax.axis_index("col"), row, valid, table)
    for j in range(tiles):
        block = lax.rem(source[j], owned)
        at = lax.rem(block, half)
        vectors[j, 0:4] = jnp.where(
            block // half == lax.axis_index(BLK[-1]),
            received[j, at].astype(jnp.float32),
            swapped[j, at].astype(jnp.float32),
        )
    rows = lax.broadcasted_iota(jnp.int32, (8, LANES), 0)

    def group(g, carry):
        found = []
        for u in range(FIRST_GROUP):
            j = g * FIRST_GROUP + u
            tile = weight[j]
            turned[j] = tile.T
            found.append((j, product(vectors, rows, j, 0, tile, 1)))
        for j, block in found:
            q = table[j]
            sums[q] = sums[q] + block
        return carry

    lax.fori_loop(0, tiles // FIRST_GROUP, group, 0)
    for s, out in enumerate((own, one, two, three)):
        out[0:owned] = sums[s * owned : (s + 1) * owned]


def multiply(table, vectors, turned, sums):
    tiles = turned.shape[0]
    sums[...] = jnp.zeros_like(sums)
    rows = lax.broadcasted_iota(jnp.int32, (8, LANES), 0)

    def group(g, carry):
        found = []
        for u in range(GROUP):
            j = g * GROUP + u
            found.append((j, product(vectors, rows, j, 0, turned[j], 0)))
        for j, block in found:
            q = table[j]
            sums[q] = sums[q] + block
        return carry

    lax.fori_loop(0, tiles // GROUP, group, 0)


def take_sums(arrived, scale, vectors):
    tiles = vectors.shape[0]
    columns = arrived.shape[0] // tiles
    blocks = jnp.sum(arrived[...].reshape(tiles, columns, 4, LANES), axis=1)
    vectors[:, 0:4, :] = blocks * scale[...]


def give_parts(outs, earlier, sums, owned):
    for s, out in enumerate(outs):
        before = earlier[s :: len(outs)]
        for t, part in enumerate(before):
            out[t * owned : (t + 1) * owned] = part[...]
        out[len(before) * owned :] = sums[s * owned : (s + 1) * owned]


def relay_kernel(cols, first, *refs):
    table, wants, arrived, *refs, vectors, sums = refs
    owned = vectors.shape[0]
    if first:
        turned, message, *parts, scale = refs
        vectors[...] = arrived[...].astype(jnp.float32)
        scale[...] = damping / vectors[:, 4:8, :]
        earlier = ()
    else:
        scale, turned, *earlier, message = refs[:-cols]
        parts = refs[-cols:]
        take_sums(arrived, scale, vectors)
    multiply(table, vectors, turned, sums)
    c = lax.axis_index("col")
    for s in range(cols):
        to = lax.rem(c + s, cols)
        for b in range(message.shape[0] // cols):
            message[b * cols + to] = sums[wants[s, b]]
    give_parts(parts, earlier, sums, owned)


def collect_kernel(table, arrived, scale, turned, own, one, two, three, vectors, sums):
    take_sums(arrived, scale, vectors)
    multiply(table, vectors, turned, sums)
    give_parts((own, one, two, three), (), sums, vectors.shape[0])


def end_tile_kernel(table, picked, turned, own, one, two, three, vectors, sums):
    owned = picked.shape[0]
    vectors[...] = picked[...].astype(jnp.float32)
    multiply(table, vectors, turned, sums)
    mass = jnp.zeros((1, LANES), jnp.float32)
    for r in (4, 5, 6):
        mass = mass + jnp.sum(vectors[:, r, :], axis=0, keepdims=True)
    for s, out in enumerate((own, one, two, three)):
        out[0:owned] = sums[s * owned : (s + 1) * owned]
        out[owned] = jnp.broadcast_to(mass, (4, LANES))


def last_kernel(own, one, two, three, total, rank_out, delta_out, masses, ordered):
    owned = total.shape[0]
    for r in range(4):
        part = slice(LANES * r, LANES * (r + 1))
        rank_out[:, part] = total[:, r, :]
        delta_out[:, part] = (
            own[0:owned, r, :] + one[0:owned, r, :] + two[0:owned, r, :] + three[0:owned, r, :]
        )
    for s, part in enumerate((own, one, two, three)):
        ordered[lax.rem(lax.axis_index("col") + 4 - s, 4)] = part[owned]
    mass = ordered[0] + ordered[1] + ordered[2] + ordered[3]
    masses[...] = mass[0:1, 0 : masses.shape[1]]


def f32(*shape):
    return jax.ShapeDtypeStruct(shape, jnp.float32)


def s32(*shape):
    return jax.ShapeDtypeStruct(shape, jnp.int32)


def call(kernel, outs, specs_in, specs_out, scratch, vmem=4, cost=None):
    return pl.pallas_call(
        kernel,
        out_shape=outs,
        in_specs=specs_in,
        out_specs=specs_out,
        scratch_shapes=scratch,
        cost_estimate=cost,
        compiler_params=pltpu.CompilerParams(vmem_limit_bytes=vmem << 20),
    )


def on_device(rank_in, delta_in, out_degree, tile_weight, tile_source, tile_row, tile_valid):
    owned, width = delta_in.shape
    tiles = tile_row.shape[0]
    n_group = lax.axis_size(BLK)
    n_column = lax.axis_size("col")
    cells = owned * n_group * n_column * width
    held = f32(owned, 4, LANES)
    message = jax.ShapeDtypeStruct((n_group, 8, LANES), jnp.bfloat16)
    block_scratch = pltpu.VMEM((owned, 4, LANES), jnp.float32)
    keep = functools.partial(pltpu.with_memory_space_constraint, memory_space=pltpu.VMEM)
    leave = functools.partial(pltpu.with_memory_space_constraint, memory_space=pltpu.HBM)
    resident = pltpu.VMEM(tile_weight.shape, tile_weight.dtype)
    indices = pltpu.SMEM((tiles,), jnp.int32)
    floats = pltpu.VMEM((owned, width), jnp.float32)
    integers = pltpu.VMEM((owned, width), jnp.int32)
    tile_scratch = [
        pltpu.VMEM((tiles, 8, LANES), jnp.float32),
        pltpu.VMEM((n_column * owned + 1, 4, LANES), jnp.float32),
    ]
    out = call(
        first_kernel,
        jax.ShapeDtypeStruct((n_group, owned // CORES + 1, 4, LANES), jnp.bfloat16),
        [HBM] * 3,
        VMEM,
        [indices, floats, integers, block_scratch, pltpu.SemaphoreType.DMA((3,))],
        cost=pl.CostEstimate(flops=40 << 30, transcendentals=0, bytes_accessed=128 << 20),
    )(leave(tile_source), leave(delta_in), leave(out_degree))
    def over_columns(parts):
        return [parts[0]] + [
            lax.ppermute(
                parts[s], "col", [(i, (i + s) % n_column) for i in range(n_column)]
            )
            for s in range(1, n_column)
        ]

    def to_groups(message):
        return lax.all_to_all(message, BLK, split_axis=0, concat_axis=0, tiled=True)

    longer = f32(owned + 1, 4, LANES)
    received = to_groups(out)
    swapped = lax.ppermute(received, BLK[-1], [(i, CORES - 1 - i) for i in range(CORES)])
    *parts, turned = call(
        functools.partial(start_tile_kernel, n_column),
        (longer,) * 4 + (resident,),
        [HBM] * 3 + [VMEM] * 3,
        (VMEM,) * 5,
        [indices] * 4 + tile_scratch + [pltpu.SemaphoreType.DMA((3,))],
    )(leave(tile_source), leave(tile_row), leave(tile_valid), received, swapped, tile_weight)
    turned = keep(turned)
    table, degrees, total, masses = call(
        functools.partial(window_kernel, n_column),
        (s32(tiles), held, held, f32(8, LANES)),
        [VMEM] + [HBM] * 5,
        (SMEM,) + (VMEM,) * 3,
        [floats, floats, integers, indices, indices, pltpu.SemaphoreType.DMA((5,))],
        cost=pl.CostEstimate(flops=0, transcendentals=0, bytes_accessed=8 << 20),
    )(
        parts[0],
        leave(delta_in),
        leave(rank_in),
        leave(out_degree),
        leave(tile_row),
        leave(tile_valid),
    )
    out, total, masses, wants = call(
        functools.partial(one_join_kernel, n_column),
        (message, held, f32(8, LANES), s32(8, LANES)),
        [VMEM] * 7,
        (VMEM,) * 4,
        [
            pltpu.VMEM((owned, 8, LANES), jnp.float32),
            pltpu.SMEM((8, LANES), jnp.int32),
            pltpu.SemaphoreType.DMA(()),
        ],
    )(*over_columns(parts), degrees, total, masses)
    arrived = to_groups(out)
    relayed = f32(n_group * n_column, 4, LANES)
    relays = range(2, ITERS - 1)
    earlier = []
    for step in relays:
        first, final = step == relays[0], step == relays[-1]
        given = (table, wants, arrived) + (() if first else (scale,)) + (turned,)
        given += tuple(earlier) if final else ()
        rows = len(relays) * owned if final else owned
        out, *parts = call(
            functools.partial(relay_kernel, n_column, first),
            (relayed,) + (f32(rows, 4, LANES),) * 4 + (held,) * first,
            [SMEM, SMEM] + [VMEM] * (len(given) - 2),
            (VMEM,) * (5 + first),
            tile_scratch,
        )(*given)
        if first:
            scale = parts.pop()
        earlier += parts
        arrived = lax.all_to_all(out, BLK_COL, split_axis=0, concat_axis=0, tiled=True)
    middle = over_columns(parts)
    parts = call(
        collect_kernel,
        (held,) * 4,
        [SMEM] + [VMEM] * 3,
        (VMEM,) * 4,
        tile_scratch,
    )(table, arrived, scale, turned)
    total, masses = call(
        functools.partial(early_join_kernel, tuple(relays)),
        (held, f32(8, LANES)),
        [VMEM] * 7,
        (VMEM,) * 2,
        [],
        cost=pl.CostEstimate(flops=0, transcendentals=0, bytes_accessed=8 << 20),
    )(parts[0], *middle, total, masses)
    out, total = call(
        functools.partial(late_join_kernel, cells),
        (message, held),
        [SMEM] + [VMEM] * 7,
        (VMEM,) * 2,
        [block_scratch],
    )(wants, *over_columns(parts), degrees, total, masses)
    parts = call(
        end_tile_kernel,
        (longer,) * 4,
        [SMEM, VMEM, VMEM],
        (VMEM,) * 4,
        tile_scratch,
    )(table, to_groups(out), turned)
    rank_out, delta_out, stacked = call(
        last_kernel,
        (f32(owned, width), f32(owned, width), f32(1, ITERS)),
        [VMEM] * 5,
        (VMEM,) * 3,
        [pltpu.VMEM((4, 4, LANES), jnp.float32)],
    )(*over_columns(parts), total)
    return rank_out, delta_out, stacked.reshape(ITERS)


def solution(mesh):
    finer = Mesh(
        mesh.devices.reshape(4, 4, 2, mesh.shape["col"]), ("blk_0", "blk_1", "blk_2", "col")
    )
    placed = (
        P(BLK_COL, None),
        P(BLK_COL, None),
        P(BLK_COL, None),
        P(BLK_COL, None, None),
        P(BLK_COL),
        P(BLK_COL),
        P(BLK_COL),
    )
    return jax.shard_map(
        on_device,
        mesh=finer,
        in_specs=placed,
        out_specs=(P(BLK_COL, None), P(BLK_COL, None), P()),
        check_vma=False,
    )
```

```python
import functools

import jax
import jax.numpy as jnp
from jax import lax
from jax.experimental import pallas as pl
from jax.experimental.pallas import tpu as pltpu
from jax.sharding import Mesh
from jax.sharding import PartitionSpec as P

ITERS = 6
BLK = ("blk_0", "blk_1", "blk_2")
BLK_COL = ("blk_0", "blk_1", "blk_2", "col")
LANES = 128
CORES = 2
LAST_GROUP = 8
GROUP = 32
FIRST_GROUP = 32

damping = 0.85

VMEM = pl.BlockSpec(memory_space=pltpu.VMEM)
SMEM = pl.BlockSpec(memory_space=pltpu.SMEM)
HBM = pl.BlockSpec(memory_space=pltpu.HBM)


def lane_row(column):
    rows = lax.broadcasted_iota(jnp.int32, column.shape, 0)
    lanes = lax.broadcasted_iota(jnp.int32, column.shape, 1)
    return jnp.sum(jnp.where(rows == lanes, column, 0.0), axis=0, keepdims=True)


def pieces(value):
    high = value.astype(jnp.bfloat16).astype(jnp.float32)
    rest = value - high
    middle = rest.astype(jnp.bfloat16).astype(jnp.float32)
    low = (rest - middle).astype(jnp.bfloat16).astype(jnp.float32)
    return high, middle, low


def targets(cols, c, row, valid, table):
    tiles = row.shape[0]
    owned = tiles

    def target(i, carry):
        block = lax.rem(row[i] // owned + cols - c, cols) * owned + lax.rem(row[i], owned)
        table[i] = jnp.where(valid[i] != 0, block, cols * owned)
        return carry

    lax.fori_loop(0, tiles, target, 0)


def started(pairs, sems):
    copies = [pltpu.make_async_copy(*pair, sems.at[i]) for i, pair in enumerate(pairs)]
    for copy in copies:
        copy.start()
    return copies


def first_kernel(source_hbm, delta_hbm, degree_hbm, message, source, delta, degree, contrib, sems):
    owned = delta.shape[0]
    for copy in started(((source_hbm, source), (delta_hbm, delta), (degree_hbm, degree)), sems):
        copy.wait()
    for r in range(4):
        part = slice(LANES * r, LANES * (r + 1))
        contrib[:, r, :] = delta[:, part] * (damping / degree[:, part].astype(jnp.float32))
    half = owned // CORES
    blocks = contrib[...].astype(jnp.bfloat16)
    for b in range(message.shape[0]):
        core = b % CORES
        message[b, 0:half] = blocks[core * half : (core + 1) * half]
        request = lax.rem(source[b], owned).astype(jnp.float32)
        message[b, half] = jnp.full((4, LANES), request, jnp.float32).astype(jnp.bfloat16)


def window_kernel(cols, *refs):
    _, delta_hbm, rank_hbm, degree_hbm, row_hbm, valid_hbm = refs[:6]
    table, degrees, total, masses = refs[6:10]
    delta_in, rank_in, degree, row, valid, sems = refs[10:]
    copies = started(
        (
            (row_hbm, row),
            (valid_hbm, valid),
            (delta_hbm, delta_in),
            (rank_hbm, rank_in),
            (degree_hbm, degree),
        ),
        sems,
    )

    for copy in copies:
        copy.wait()
    targets(cols, lax.axis_index("col"), row, valid, table)
    mass = jnp.zeros((1, LANES), jnp.float32)
    for r in range(4):
        part = slice(LANES * r, LANES * (r + 1))
        delta = delta_in[:, part]
        degrees[:, r, :] = degree[:, part].astype(jnp.float32)
        total[:, r, :] = rank_in[:, part] + delta
        mass = mass + jnp.sum(jnp.abs(delta), axis=0, keepdims=True)
    masses[...] = jnp.concatenate([mass, jnp.zeros((7, LANES), jnp.float32)], axis=0)


def one_join_kernel(cols, own, one, two, three, degrees, total, masses, *refs):
    message, total_out, masses_out, wants, contrib, asked, sem = refs
    owned = total.shape[0]
    parts = (own, one, two, three)
    for s, part in enumerate(parts):
        at = (cols - s) % cols
        wants[at : at + 1, :] = part[owned, 0:1, :].astype(jnp.int32) + at * owned
    copy = pltpu.make_async_copy(wants, asked, sem)
    copy.start()
    delta = own[0:owned] + one[0:owned] + two[0:owned] + three[0:owned]
    total_out[...] = total[...] + delta
    contrib[:, 0:4, :] = delta * (damping / degrees[...])
    contrib[:, 4:8, :] = degrees[...]
    mass = jnp.sum(jnp.sum(jnp.abs(delta), axis=0), axis=0, keepdims=True)
    rows = lax.broadcasted_iota(jnp.int32, (8, LANES), 0)
    masses_out[...] = jnp.where(rows == 1, mass, masses[...])
    copy.wait()
    for b in range(message.shape[0]):
        message[b] = contrib[asked[0, b]].astype(jnp.bfloat16)


def tally(steps, own, one, two, three, total, masses):
    owned = total.shape[0]
    ranks = total[...]
    merged = masses[...]
    rows = lax.broadcasted_iota(jnp.int32, (8, LANES), 0)
    for t, step in enumerate(steps):
        part = slice(t * owned, (t + 1) * owned)
        delta = own[part] + one[part] + two[part] + three[part]
        ranks = ranks + delta
        mass = jnp.sum(jnp.sum(jnp.abs(delta), axis=0), axis=0, keepdims=True)
        merged = jnp.where(rows == step, mass, merged)
    return ranks, merged, delta


def early_join_kernel(steps, _, own, one, two, three, total, masses, total_out, masses_out):
    total_out[...], masses_out[...], _ = tally(steps, own, one, two, three, total, masses)


def late_join_kernel(cells, wants, own, one, two, three, degrees, total, masses, *refs):
    message, total_out, contrib = refs
    total_out[...], merged, delta = tally((ITERS - 1,), own, one, two, three, total, masses)
    contrib[...] = delta * (damping / degrees[...])
    sums = jnp.broadcast_to(jnp.sum(merged, axis=1, keepdims=True) / cells, (8, LANES))
    extra = jnp.concatenate([*pieces(lane_row(sums)), jnp.zeros((1, LANES), jnp.float32)], axis=0)
    for b in range(message.shape[0]):
        message[b] = jnp.concatenate([contrib[wants[0, b]], extra], axis=0).astype(jnp.bfloat16)


def product(vectors, rows, j, first, weight, contracted):
    wide = jnp.concatenate(
        [jnp.broadcast_to(vectors[j, first + r][None], (8, LANES)) for r in range(4)], axis=1
    )
    found = lax.dot_general(
        wide.astype(jnp.bfloat16),
        weight,
        (((1,), (contracted,)), ((), ())),
        preferred_element_type=jnp.float32,
    )
    block = found[:, 3 * LANES :]
    for r in (2, 1, 0):
        block = jnp.where(rows == r, found[:, LANES * r : LANES * (r + 1)], block)
    return block[:4]


def start_tile_kernel(cols, *refs):
    source_hbm, row_hbm, valid_hbm, received, swapped, weight = refs[:6]
    own, one, two, three, turned = refs[6:11]
    source, row, valid, table, vectors, sums, small_sems = refs[11:]
    tiles = weight.shape[0]
    owned = tiles

    copies = started(((source_hbm, source), (row_hbm, row), (valid_hbm, valid)), small_sems)
    sums[...] = jnp.zeros_like(sums)
    asking = lax.broadcasted_iota(jnp.int32, (tiles, LANES), 0)
    lanes = lax.broadcasted_iota(jnp.int32, (tiles, LANES), 1)
    half = owned // CORES
    requests = received[:, half, :, :].astype(jnp.float32)[:, 0, :]
    asked = jnp.sum(jnp.where(asking == lanes, requests, 0.0), axis=0, keepdims=True)
    for out in (own, one, two, three):
        out[owned] = jnp.broadcast_to(asked, (4, LANES))
    for copy in copies:
        copy.wait()
    targets(cols, lax.axis_index("col"), row, valid, table)
    for j in range(tiles):
        block = lax.rem(source[j], owned)
        at = lax.rem(block, half)
        vectors[j, 0:4] = jnp.where(
            block // half == lax.axis_index(BLK[-1]),
            received[j, at].astype(jnp.float32),
            swapped[j, at].astype(jnp.float32),
        )
    rows = lax.broadcasted_iota(jnp.int32, (8, LANES), 0)

    def group(g, carry):
        found = []
        for u in range(FIRST_GROUP):
            j = g * FIRST_GROUP + u
            tile = weight[j]
            turned[j] = tile.T
            found.append((j, product(vectors, rows, j, 0, tile, 1)))
        for j, block in found:
            q = table[j]
            sums[q] = sums[q] + block
        return carry

    lax.fori_loop(0, tiles // FIRST_GROUP, group, 0)
    for s, out in enumerate((own, one, two, three)):
        out[0:owned] = sums[s * owned : (s + 1) * owned]


def multiply(table, vectors, turned, sums):
    tiles = turned.shape[0]
    sums[...] = jnp.zeros_like(sums)
    rows = lax.broadcasted_iota(jnp.int32, (8, LANES), 0)

    def group(g, carry):
        found = []
        for u in range(GROUP):
            j = g * GROUP + u
            found.append((j, product(vectors, rows, j, 0, turned[j], 0)))
        for j, block in found:
            q = table[j]
            sums[q] = sums[q] + block
        return carry

    lax.fori_loop(0, tiles // GROUP, group, 0)


def take_sums(arrived, scale, vectors):
    tiles = vectors.shape[0]
    columns = arrived.shape[0] // tiles
    blocks = jnp.sum(arrived[...].reshape(tiles, columns, 4, LANES), axis=1)
    vectors[:, 0:4, :] = blocks * scale[...]


def give_parts(outs, earlier, sums, owned):
    for s, out in enumerate(outs):
        before = earlier[s :: len(outs)]
        for t, part in enumerate(before):
            out[t * owned : (t + 1) * owned] = part[...]
        out[len(before) * owned :] = sums[s * owned : (s + 1) * owned]


def relay_kernel(cols, first, *refs):
    table, wants, arrived, *refs, vectors, sums = refs
    owned = vectors.shape[0]
    if first:
        turned, message, *parts, scale = refs
        vectors[...] = arrived[...].astype(jnp.float32)
        scale[...] = damping / vectors[:, 4:8, :]
        earlier = ()
    else:
        scale, turned, *earlier, message = refs[:-cols]
        parts = refs[-cols:]
        take_sums(arrived, scale, vectors)
    multiply(table, vectors, turned, sums)
    c = lax.axis_index("col")
    for s in range(cols):
        to = lax.rem(c + s, cols)
        for b in range(message.shape[0] // cols):
            message[b * cols + to] = sums[wants[s, b]]
    give_parts(parts, earlier, sums, owned)


def collect_kernel(table, arrived, scale, turned_hbm, own, one, two, three, turned, vectors, sums, sems):
    tiles = turned.shape[0]

    def fetch(j):
        return pltpu.make_async_copy(turned_hbm.at[j], turned.at[j], sems.at[j])

    for j in range(tiles):
        fetch(j).start(priority=j % 2)
    take_sums(arrived, scale, vectors)
    sums[...] = jnp.zeros_like(sums)
    rows = lax.broadcasted_iota(jnp.int32, (8, LANES), 0)
    for g in range(0, tiles, LAST_GROUP):
        found = []
        for j in range(g, g + LAST_GROUP):
            fetch(j).wait()
        for j in range(g, g + LAST_GROUP):
            found.append((j, product(vectors, rows, j, 0, turned[j], 0)))
        for j, block in found:
            q = table[j]
            sums[q] = sums[q] + block
    give_parts((own, one, two, three), (), sums, vectors.shape[0])


def end_tile_kernel(table, picked, turned, own, one, two, three, vectors, sums):
    owned = picked.shape[0]
    vectors[...] = picked[...].astype(jnp.float32)
    multiply(table, vectors, turned, sums)
    mass = jnp.zeros((1, LANES), jnp.float32)
    for r in (4, 5, 6):
        mass = mass + jnp.sum(vectors[:, r, :], axis=0, keepdims=True)
    for s, out in enumerate((own, one, two, three)):
        out[0:owned] = sums[s * owned : (s + 1) * owned]
        out[owned] = jnp.broadcast_to(mass, (4, LANES))


def last_kernel(own, one, two, three, total, rank_out, delta_out, masses, ordered):
    owned = total.shape[0]
    for r in range(4):
        part = slice(LANES * r, LANES * (r + 1))
        rank_out[:, part] = total[:, r, :]
        delta_out[:, part] = (
            own[0:owned, r, :] + one[0:owned, r, :] + two[0:owned, r, :] + three[0:owned, r, :]
        )
    for s, part in enumerate((own, one, two, three)):
        ordered[lax.rem(lax.axis_index("col") + 4 - s, 4)] = part[owned]
    mass = ordered[0] + ordered[1] + ordered[2] + ordered[3]
    masses[...] = mass[0:1, 0 : masses.shape[1]]


def f32(*shape):
    return jax.ShapeDtypeStruct(shape, jnp.float32)


def s32(*shape):
    return jax.ShapeDtypeStruct(shape, jnp.int32)


def call(kernel, outs, specs_in, specs_out, scratch, vmem=4, cost=None):
    return pl.pallas_call(
        kernel,
        out_shape=outs,
        in_specs=specs_in,
        out_specs=specs_out,
        scratch_shapes=scratch,
        cost_estimate=cost,
        compiler_params=pltpu.CompilerParams(vmem_limit_bytes=vmem << 20),
    )


def on_device(rank_in, delta_in, out_degree, tile_weight, tile_source, tile_row, tile_valid):
    owned, width = delta_in.shape
    tiles = tile_row.shape[0]
    n_group = lax.axis_size(BLK)
    n_column = lax.axis_size("col")
    cells = owned * n_group * n_column * width
    held = f32(owned, 4, LANES)
    message = jax.ShapeDtypeStruct((n_group, 8, LANES), jnp.bfloat16)
    block_scratch = pltpu.VMEM((owned, 4, LANES), jnp.float32)
    keep = functools.partial(pltpu.with_memory_space_constraint, memory_space=pltpu.VMEM)
    leave = functools.partial(pltpu.with_memory_space_constraint, memory_space=pltpu.HBM)
    resident = pltpu.VMEM(tile_weight.shape, tile_weight.dtype)
    indices = pltpu.SMEM((tiles,), jnp.int32)
    floats = pltpu.VMEM((owned, width), jnp.float32)
    integers = pltpu.VMEM((owned, width), jnp.int32)
    tile_scratch = [
        pltpu.VMEM((tiles, 8, LANES), jnp.float32),
        pltpu.VMEM((n_column * owned + 1, 4, LANES), jnp.float32),
    ]
    out = call(
        first_kernel,
        jax.ShapeDtypeStruct((n_group, owned // CORES + 1, 4, LANES), jnp.bfloat16),
        [HBM] * 3,
        VMEM,
        [indices, floats, integers, block_scratch, pltpu.SemaphoreType.DMA((3,))],
        cost=pl.CostEstimate(flops=40 << 30, transcendentals=0, bytes_accessed=128 << 20),
    )(leave(tile_source), leave(delta_in), leave(out_degree))
    def over_columns(parts):
        return [parts[0]] + [
            lax.ppermute(
                parts[s], "col", [(i, (i + s) % n_column) for i in range(n_column)]
            )
            for s in range(1, n_column)
        ]

    def to_groups(message):
        return lax.all_to_all(message, BLK, split_axis=0, concat_axis=0, tiled=True)

    longer = f32(owned + 1, 4, LANES)
    received = to_groups(out)
    swapped = lax.ppermute(received, BLK[-1], [(i, CORES - 1 - i) for i in range(CORES)])
    *parts, turned = call(
        functools.partial(start_tile_kernel, n_column),
        (longer,) * 4 + (resident,),
        [HBM] * 3 + [VMEM] * 3,
        (VMEM,) * 5,
        [indices] * 4 + tile_scratch + [pltpu.SemaphoreType.DMA((3,))],
    )(leave(tile_source), leave(tile_row), leave(tile_valid), received, swapped, tile_weight)
    unplaced = turned
    turned = keep(turned)
    table, degrees, total, masses = call(
        functools.partial(window_kernel, n_column),
        (s32(tiles), held, held, f32(8, LANES)),
        [VMEM] + [HBM] * 5,
        (SMEM,) + (VMEM,) * 3,
        [floats, floats, integers, indices, indices, pltpu.SemaphoreType.DMA((5,))],
        cost=pl.CostEstimate(flops=0, transcendentals=0, bytes_accessed=8 << 20),
    )(
        parts[0],
        leave(delta_in),
        leave(rank_in),
        leave(out_degree),
        leave(tile_row),
        leave(tile_valid),
    )
    out, total, masses, wants = call(
        functools.partial(one_join_kernel, n_column),
        (message, held, f32(8, LANES), s32(8, LANES)),
        [VMEM] * 7,
        (VMEM,) * 4,
        [
            pltpu.VMEM((owned, 8, LANES), jnp.float32),
            pltpu.SMEM((8, LANES), jnp.int32),
            pltpu.SemaphoreType.DMA(()),
        ],
    )(*over_columns(parts), degrees, total, masses)
    arrived = to_groups(out)
    relayed = f32(n_group * n_column, 4, LANES)
    relays = range(2, ITERS - 1)
    earlier = []
    for step in relays:
        first, final = step == relays[0], step == relays[-1]
        given = (table, wants, arrived) + (() if first else (scale,)) + (turned,)
        given += tuple(earlier) if final else ()
        rows = len(relays) * owned if final else owned
        out, *parts = call(
            functools.partial(relay_kernel, n_column, first),
            (relayed,) + (f32(rows, 4, LANES),) * 4 + (held,) * first,
            [SMEM, SMEM] + [VMEM] * (len(given) - 2),
            (VMEM,) * (5 + first),
            tile_scratch,
        )(*given)
        if first:
            scale = parts.pop()
        earlier += parts
        arrived = lax.all_to_all(out, BLK_COL, split_axis=0, concat_axis=0, tiled=True)
    middle = over_columns(parts)
    *parts, turned = call(
        collect_kernel,
        (held,) * 4 + (resident,),
        [SMEM] + [VMEM] * 2 + [HBM],
        (VMEM,) * 5,
        tile_scratch + [pltpu.SemaphoreType.DMA((tiles,))],
    )(table, arrived, scale, leave(unplaced))
    total, masses = call(
        functools.partial(early_join_kernel, tuple(relays)),
        (held, f32(8, LANES)),
        [VMEM] * 7,
        (VMEM,) * 2,
        [],
        cost=pl.CostEstimate(flops=0, transcendentals=0, bytes_accessed=8 << 20),
    )(parts[0], *middle, total, masses)
    out, total = call(
        functools.partial(late_join_kernel, cells),
        (message, held),
        [SMEM] + [VMEM] * 7,
        (VMEM,) * 2,
        [block_scratch],
    )(wants, *over_columns(parts), degrees, total, masses)
    parts = call(
        end_tile_kernel,
        (longer,) * 4,
        [SMEM, VMEM, VMEM],
        (VMEM,) * 4,
        tile_scratch,
    )(table, to_groups(out), keep(turned))
    rank_out, delta_out, stacked = call(
        last_kernel,
        (f32(owned, width), f32(owned, width), f32(1, ITERS)),
        [VMEM] * 5,
        (VMEM,) * 3,
        [pltpu.VMEM((4, 4, LANES), jnp.float32)],
    )(*over_columns(parts), total)
    return rank_out, delta_out, stacked.reshape(ITERS)


def solution(mesh):
    finer = Mesh(
        mesh.devices.reshape(4, 4, 2, mesh.shape["col"]), ("blk_0", "blk_1", "blk_2", "col")
    )
    placed = (
        P(BLK_COL, None),
        P(BLK_COL, None),
        P(BLK_COL, None),
        P(BLK_COL, None, None),
        P(BLK_COL),
        P(BLK_COL),
        P(BLK_COL),
    )
    return jax.shard_map(
        on_device,
        mesh=finer,
        in_specs=placed,
        out_specs=(P(BLK_COL, None), P(BLK_COL, None), P()),
        check_vma=False,
    )
```
